32 devices in a mesh: dp: 8 (over z, y), mp: 4 (over x, core).
Axes of the slice: x: 2, y: 2, z: 4, core: 2. Of those that a mesh axis runs over, the one named last changes fastest.
Arguments:
- residual: bfloat16 [16384, 768], P('dp', 'mp'), may hold values from -6 to 6, as said below
- lengths: int32 [8, 4], P('dp'), may hold values from 0 to 2048, as said below
- gain_one: float32 [768], P('mp'), may hold values from 0.5 to 1.5
- input_weight: bfloat16 [3, 768, 768], P(None, None, 'mp'), may hold values from -0.21875 to 0.21875
- input_bias: float32 [2, 768], P(None, 'mp'), may hold values from -1.8 to 1.8
- output_weight: bfloat16 [768, 768], P('mp'), may hold values from -2.5 to 2.5
- output_bias: float32 [768], P('mp'), may hold values from -1.8 to 1.8
- gain_two: float32 [768], P('mp'), may hold values from 0.5 to 1.5
- expand_weight: bfloat16 [768, 3072], P(None, 'mp'), may hold values from -0.21875 to 0.21875
- expand_bias: float32 [3072], P('mp'), may hold values from -1.8 to 1.8
- reduce_weight: bfloat16 [3072, 768], P('mp'), may hold values from -0.109375 to 0.109375
- reduce_bias: float32 [768], P('mp'), may hold values from -1.8 to 1.8
- cotangent: bfloat16 [16384, 768], P('dp', 'mp'), may hold values from -6 to 6
Outputs:
- residual_out: bfloat16 [16384, 768], P('dp', 'mp')
- residual_grad: bfloat16 [16384, 768], P('dp', 'mp')
- input_weight_grad: float32 [3, 768, 768], P(None, None, 'mp')
- input_bias_grad: float32 [2, 768], P(None, 'mp')
- output_weight_grad: float32 [768, 768], P('mp')
- output_bias_grad: float32 [768], P('mp')
- gain_one_grad: float32 [768], P('mp')
- gain_two_grad: float32 [768], P('mp')
- expand_weight_grad: float32 [768, 3072], P(None, 'mp')
- expand_bias_grad: float32 [3072], P('mp')
- reduce_weight_grad: float32 [3072, 768], P('mp')
- reduce_bias_grad: float32 [768], P('mp')
- residual_rms: float32 [], replicated
- live_count: int32 [], replicated
The draws below stay inside these ranges and needn't reach their ends.
Inputs may be any that keep to these rules, and one draw needn't show every extreme that they name: Each row holds one group's sequence lengths by slot: first some of 2048, then some of 512, then zeros for unused slots; a row sums to at most 2048, and the first row holds a sequence of 2048. `residual`: column 767 is not read.
All inputs are finite; a program needn't handle non-finite values.
Results may differ from the reference program's by a relative error of at most 0.015.
Values may be sent and summed in bfloat16 or wider, within the bound.
A program may use at most 128 MiB of HBM per device.

```python
import jax
import jax.numpy as jnp
from jax import lax

D = 768
HEADS = 12
HEAD = 64
FF = 3072
SHORT = 512
LONG = 2048
TOK_DEV = 2048
GROUPS = 8
SLOTS = 4
TOKENS = 16384


def draw_residual(key, part):
    raw = jnp.clip(jax.random.normal(key, (TOKENS, D), jnp.float32), -5.0, 5.0)
    centered = raw - jnp.mean(raw, axis=1, keepdims=True)
    return jnp.clip(centered, -6.0, 6.0).astype(jnp.bfloat16)


def draw_lengths(key, part):
    first_key, second_key = jax.random.split(key)
    per_long = LONG // SHORT
    longs = jax.random.randint(first_key, (GROUPS,), 0, TOK_DEV // LONG + 1)
    longs = jnp.maximum(longs, (jnp.arange(GROUPS) == 0).astype(jnp.int32))
    room = SLOTS - longs * per_long
    shorts = jax.random.randint(second_key, (GROUPS,), 0, room + 1)
    positions = jnp.arange(SLOTS)[None, :]
    chosen = jnp.where(positions < longs[:, None], LONG, jnp.where(positions < (longs + shorts)[:, None], SHORT, 0))
    return chosen.astype(jnp.int32)


def block_levels(stream_key, shape, cuts, smallest, largest):
    def one(dim, shards_of):
        heights = jax.random.uniform(jax.random.fold_in(jax.random.fold_in(stream_key, 6), dim), (shards_of,), jnp.float32, smallest / len(cuts), largest / len(cuts))
        return jnp.repeat(jnp.exp(heights), shape[dim] // shards_of).reshape((-1,) + (1,) * (len(shape) - dim - 1))

    level = one(*cuts[0])
    for cut in cuts[1:]:
        level = level * one(*cut)
    return level


def scatter_about(stream_key, shape, spread, reach, cuts=(), dtype=jnp.bfloat16):
    values = spread * jax.random.normal(stream_key, shape, jnp.float32)
    if cuts:
        values = values * block_levels(stream_key, shape, cuts, -0.22, 0.18)
    return jnp.clip(values, -reach, reach).astype(dtype)


def setup_inputs(seed: int = 0) -> dict:
    key_of = jax.random.split(jax.random.key(seed), 14)
    return {
        "residual": draw_residual(jax.random.fold_in(key_of[13], 71), 0),
        "lengths": draw_lengths(jax.random.fold_in(key_of[13], 71), 0),
        "gain_one": jnp.clip(1.0 + 0.1 * jax.random.normal(key_of[2], (D,), jnp.float32), 0.5, 1.5),
        "input_weight": scatter_about(key_of[3], (3, D, D), D ** -0.5, 0.21875, ((2, 4),)),
        "input_bias": scatter_about(key_of[4], (2, D), 0.3, 1.8, ((1, 4),), jnp.float32),
        "output_weight": scatter_about(key_of[5], (D, D), (max(D // 128, 1)) ** -0.5, 2.5, ((0, 4),)),
        "output_bias": scatter_about(key_of[6], (D,), 0.3, 1.8, ((0, 4),), jnp.float32),
        "gain_two": jnp.clip(1.0 + 0.1 * jax.random.normal(key_of[7], (D,), jnp.float32), 0.5, 1.5),
        "expand_weight": scatter_about(key_of[8], (D, FF), D ** -0.5, 0.21875, ((1, 4),)),
        "expand_bias": scatter_about(key_of[9], (FF,), 0.3, 1.8, ((0, 4),), jnp.float32),
        "reduce_weight": scatter_about(key_of[10], (FF, D), FF ** -0.5, 0.109375, ((0, 4),)),
        "reduce_bias": scatter_about(key_of[11], (D,), 0.3, 1.8, ((0, 4),), jnp.float32),
        "cotangent": scatter_about(key_of[12], (TOKENS, D), 1.0, 6.0, ((0, 8), (1, 4))),
    }


EPSILON = 1e-05
SCORE_SCALE = 0.125
NEGATIVE = -1e+30
HIGHEST_PRECISION = lax.Precision.HIGHEST

@jax.custom_vjp
def low(v):
    return lax.optimization_barrier(v.astype(jnp.bfloat16)).astype(jnp.float32)

@jax.custom_vjp
def low_back(v):
    return v

def low_keep(v):
    return (low(v), None)

def low_pass(kept, grad):
    return (grad,)

def back_keep(v):
    return (v, None)

def back_low(kept, grad):
    return (low(grad),)
low.defvjp(low_keep, low_pass)
low_back.defvjp(back_keep, back_low)

def matmul(left_side, right_side):
    return jnp.dot(left_side, right_side, precision=HIGHEST_PRECISION)

def compressed_norm(values, gain_vec):
    implied = -lax.optimization_barrier(jnp.sum(values, axis=1, keepdims=True))
    decompressed = jnp.concatenate([values, implied], axis=1)
    inverse = lax.rsqrt(lax.optimization_barrier(jnp.mean(decompressed * decompressed, axis=1, keepdims=True)) + EPSILON)
    return decompressed * inverse * gain_vec

def segments(seq_lengths, row_count):
    seq_ends = jnp.cumsum(seq_lengths).astype(jnp.int32)
    positions = jnp.arange(row_count).astype(jnp.int32)
    segment = lax.optimization_barrier(jnp.sum((positions[:, None] >= seq_ends[None, :]).astype(jnp.int32), axis=1))
    return (segment, positions < seq_ends[-1])

def window(row_start, row_count, segment, live_rows):
    key_start = jnp.clip(row_start + SHORT - LONG, 0, row_count - LONG).astype(jnp.int32)
    query_pos = row_start + jnp.arange(SHORT).astype(jnp.int32)
    key_pos = key_start + jnp.arange(LONG).astype(jnp.int32)
    query_seg = lax.dynamic_slice_in_dim(segment, row_start, SHORT)
    key_seg = lax.dynamic_slice_in_dim(segment, key_start, LONG)
    query_live = lax.dynamic_slice_in_dim(live_rows, row_start, SHORT)
    causal = key_pos[None, :] <= query_pos[:, None]
    allowed = (query_seg[:, None] == key_seg[None, :]) & causal & query_live[:, None]
    return (key_start, allowed | (key_pos[None, :] == query_pos[:, None]))

def attend(queries, key_rows, value_rows, segment, live_rows):
    row_count = queries.shape[0]

    def attend_block(block_index):
        row_start = block_index * SHORT
        key_start, allowed = window(row_start, row_count, segment, live_rows)
        query_block = lax.dynamic_slice_in_dim(queries, row_start, SHORT, 0)
        key_block = lax.dynamic_slice_in_dim(key_rows, key_start, LONG, 0)
        value_block = lax.dynamic_slice_in_dim(value_rows, key_start, LONG, 0)
        scores = low_back(jnp.einsum('qhd,khd->hqk', query_block, key_block, precision=HIGHEST_PRECISION) * SCORE_SCALE)
        scores = jnp.where(allowed[None], scores, NEGATIVE)
        attn_probs = low(jax.nn.softmax(scores, axis=2))
        return jnp.einsum('hqk,khd->qhd', attn_probs, value_block, precision=HIGHEST_PRECISION)
    blocks = lax.map(jax.checkpoint(attend_block), jnp.arange(row_count // SHORT).astype(jnp.int32))
    return blocks.reshape(row_count, HEADS * HEAD)

def layer_forward(values, weights, segment, live_rows):
    gain_one, input_weight, input_bias, output_weight, output_bias, gain_two, expand_weight, expand_bias, reduce_weight, reduce_bias = weights
    row_count = values.shape[0]
    rows_one = low(compressed_norm(values, gain_one))
    projected = jnp.einsum('td,cde->cte', rows_one, input_weight, precision=HIGHEST_PRECISION)
    queries = low(low_back(projected[0] + input_bias[0])).reshape(row_count, HEADS, HEAD)
    key_rows = low(low_back(projected[1])).reshape(row_count, HEADS, HEAD)
    value_rows = low(low_back(projected[2] + input_bias[1])).reshape(row_count, HEADS, HEAD)
    mixed = low(low_back(attend(queries, key_rows, value_rows, segment, live_rows)))
    branch_one = low_back(matmul(mixed, output_weight)) + output_bias
    values_one = values + branch_one[:, :D - 1] - lax.optimization_barrier(jnp.mean(branch_one, axis=1, keepdims=True))
    rows_two = low(compressed_norm(values_one, gain_two))
    hidden = low_back(matmul(rows_two, expand_weight) + expand_bias)
    active = low(jax.nn.gelu(hidden, approximate=True))
    branch_two = low_back(matmul(active, reduce_weight)) + reduce_bias
    return values_one + branch_two[:, :D - 1] - lax.optimization_barrier(jnp.mean(branch_two, axis=1, keepdims=True))

def reference(residual, lengths, gain_one, input_weight, input_bias, output_weight, output_bias, gain_two, expand_weight, expand_bias, reduce_weight, reduce_bias, cotangent):
    params = tuple((array.astype(jnp.float32) for array in (gain_one, input_weight, input_bias, output_weight, output_bias, gain_two, expand_weight, expand_bias, reduce_weight, reduce_bias)))
    row_count = residual.shape[0] // GROUPS
    inputs = residual.astype(jnp.float32).reshape(GROUPS, row_count, D)[:, :, :D - 1]
    cotangents = cotangent.astype(jnp.float32).reshape(GROUPS, row_count, D)[:, :, :D - 1]

    def group_step(running, group_item):
        values, group_cot, seq_lengths = group_item
        segment, live_rows = segments(seq_lengths, row_count)

        def forward_fn(inner_values, *weights):
            return layer_forward(inner_values, weights, segment, live_rows)
        result, pullback = jax.vjp(forward_fn, values, *params)
        gradients = pullback(group_cot)
        weight_sums, square_sum = running
        weight_sums = tuple((total + grad for total, grad in zip(weight_sums, gradients[1:])))
        per_token = lax.optimization_barrier(jnp.sum(result * result, axis=1)) + lax.optimization_barrier(jnp.sum(result, axis=1)) ** 2
        square_sum = square_sum + jnp.sum(jnp.where(live_rows, per_token, 0.0))
        return ((weight_sums, square_sum), (result, gradients[0]))
    start = (tuple((jnp.zeros_like(param) for param in params)), jnp.zeros((), jnp.float32))
    (weight_sums, square_sum), (results, input_grads) = lax.scan(group_step, start, (inputs, cotangents, lengths))
    zero_col = jnp.zeros((GROUPS, row_count, 1), jnp.float32)
    residual_out = jnp.concatenate([results, zero_col], axis=2).reshape(-1, D).astype(jnp.bfloat16)
    residual_grad = jnp.concatenate([input_grads, zero_col], axis=2).reshape(-1, D).astype(jnp.bfloat16)
    live_count = jnp.sum(lengths).astype(jnp.int32)
    residual_rms = jnp.sqrt(square_sum / (D * live_count.astype(jnp.float32)))
    gain_one_grad, input_weight_grad, input_bias_grad, output_weight_grad, output_bias_grad, gain_two_grad, expand_weight_grad, expand_bias_grad, reduce_weight_grad, reduce_bias_grad = weight_sums
    return (residual_out, residual_grad, input_weight_grad, input_bias_grad, output_weight_grad, output_bias_grad, gain_one_grad, gain_two_grad, expand_weight_grad, expand_bias_grad, reduce_weight_grad, reduce_bias_grad, residual_rms, live_count)
```

```python
import functools

import jax
import jax.numpy as jnp
from jax import lax
from jax.experimental import pallas as pl
from jax.experimental.pallas import tpu as pltpu
from jax.sharding import PartitionSpec as P

D = 768
HEAD = 64
SHORT = 512
LONG = 2048
EPSILON = 1e-05
SCORE_SCALE = 0.125
FAR = 1e30

F32 = jnp.float32
BF16 = jnp.bfloat16
VMEM = pltpu.VMEM
SMEM = pltpu.SMEM
NT = (((1,), (1,)), ((), ()))
TN = (((0,), (0,)), ((), ()))


def dot(a, b):
    return jnp.dot(a, b, preferred_element_type=F32)


def dot_nt(a, b):
    return lax.dot_general(a, b, NT, preferred_element_type=F32)


def dot_tn(a, b):
    return lax.dot_general(a, b, TN, preferred_element_type=F32)


def lanes(shape):
    return lax.broadcasted_iota(jnp.int32, shape, 1)


def rows_of(shape):
    return lax.broadcasted_iota(jnp.int32, shape, 0)


def decompress(raw):
    pad = lanes(raw.shape) == D - 1
    kept = jnp.where(pad, 0.0, raw)
    full = jnp.where(pad, -jnp.sum(kept, axis=1, keepdims=True), kept)
    inverse = lax.rsqrt(jnp.mean(full * full, axis=1, keepdims=True) + EPSILON)
    return full, inverse


def center(rows):
    return rows - jnp.mean(rows, axis=1, keepdims=True)


def branch_grad(raw):
    pad = lanes(raw.shape) == D - 1
    return center(jnp.where(pad, 0.0, raw))


def head_of(values, head):
    return jnp.where(lanes(values.shape) // HEAD == head, values, jnp.zeros_like(values))


def flags(lengths_ref):
    total = lengths_ref[0, 0]
    for slot in range(1, lengths_ref.shape[1]):
        total = total + lengths_ref[0, slot]
    return lengths_ref[0, 0] == LONG, total


def diagonal(live, transposed):
    a = rows_of((SHORT, SHORT))
    b = lanes((SHORT, SHORT))
    query, key = (b, a) if transposed else (a, b)
    return (key == query) | ((key < query) & live)


def forward_kernel(
    lengths_ref, res_ref, gain_ref, w_ref, bias_ref,
    q_ref, k_ref, v_ref, mixed_ref, lse_ref, k_s, v_s,
):
    i = pl.program_id(0)
    heads = q_ref.shape[1] // HEAD
    width = q_ref.shape[1]
    full, inverse = decompress(res_ref[...].astype(F32))
    rows = (full * inverse * gain_ref[...]).astype(BF16)
    q = (dot(rows, w_ref[0]) + bias_ref[0:1]).astype(BF16)
    k = dot(rows, w_ref[1]).astype(BF16)
    v = (dot(rows, w_ref[2]) + bias_ref[1:2]).astype(BF16)
    q_ref[...] = q
    k_ref[...] = k
    v_ref[...] = v
    v_ext = jnp.concatenate([v, jnp.ones((SHORT, HEAD), BF16)], axis=1)
    here = pl.ds(pl.multiple_of(i * SHORT, SHORT), SHORT)
    k_s[here] = k
    v_s[here] = v_ext
    is_long, total = flags(lengths_ref)
    live = i * SHORT < total
    far = jnp.where(is_long, 0.0, FAR)
    allowed = diagonal(live, False)
    scaled = q * SCORE_SCALE
    q_heads = [head_of(scaled, h) for h in range(heads)]

    carry = []
    for h in range(heads):
        s = jnp.where(allowed, dot_nt(q_heads[h], k), -FAR)
        m = jnp.max(s, axis=1, keepdims=True)
        p = jnp.exp(s - m).astype(BF16)
        carry.append((m, dot(p, v_ext)))

    def body(j, carry):
        there = pl.ds(pl.multiple_of(j * SHORT, SHORT), SHORT)
        k_j = k_s[there]
        v_j = v_s[there]
        out = []
        for h in range(heads):
            m, acc = carry[h]
            s = dot_nt(q_heads[h], k_j)
            new = jnp.maximum(m, jnp.max(s, axis=1, keepdims=True) - far)
            p = jnp.exp(s - (new + far)).astype(BF16)
            out.append((new, acc * jnp.exp(m - new) + dot(p, v_j)))
        return out

    carry = lax.fori_loop(0, i, body, carry)
    mixed = jnp.zeros((SHORT, width), F32)
    lse = jnp.zeros((SHORT, 128), F32)
    for h in range(heads):
        m, acc = carry[h]
        norm = acc[:, width : width + 1]
        mixed = mixed + head_of(acc[:, :width] / norm, h)
        lse = jnp.where(lanes(lse.shape) == h, m + jnp.log(norm), lse)
    mixed_ref[...] = mixed.astype(BF16)
    lse_ref[...] = jnp.transpose(lse)[:8]


def middle_kernel(
    res_ref, cot_ref, mixed_ref, wo_ref, bo_ref, gain_ref, we_ref, be_ref, wr_ref,
    x1_ref, b2_ref, e2_ref, gwe_ref, gwr_ref, gbe_ref, gbr_ref, gwe_s, gwr_s,
):
    i = pl.program_id(0)

    @pl.when(i == 0)
    def _():
        gwe_s[...] = jnp.zeros_like(gwe_s)
        gwr_s[...] = jnp.zeros_like(gwr_s)
        gbe_ref[...] = jnp.zeros_like(gbe_ref)
        gbr_ref[...] = jnp.zeros_like(gbr_ref)

    full, _ = decompress(res_ref[...].astype(F32))
    x1 = full + center(dot(mixed_ref[...], wo_ref[...]) + bo_ref[...])
    x1_ref[...] = x1
    inverse = lax.rsqrt(jnp.mean(x1 * x1, axis=1, keepdims=True) + EPSILON)
    rows = (x1 * inverse * gain_ref[...]).astype(BF16)
    z = dot(rows, we_ref[...]) + be_ref[...]
    t = jnp.tanh(0.7978845608 * (z + 0.044715 * (z * z * z)))
    active = (0.5 * z * (1.0 + t)).astype(BF16)
    slope = 0.5 * (1.0 + t) + 0.5 * z * (1.0 - t * t) * (
        0.7978845608 * (1.0 + (3 * 0.044715) * (z * z))
    )
    b2_ref[...] = center(dot(active, wr_ref[...])).astype(BF16)
    g2 = branch_grad(cot_ref[...].astype(F32))
    gbr_ref[...] += jnp.sum(g2, axis=0, keepdims=True)
    g2 = g2.astype(BF16)
    gwr_s[...] += dot_tn(active, g2)
    d_hidden = (dot_nt(g2, wr_ref[...]) * slope).astype(BF16)
    gbe_ref[...] += jnp.sum(d_hidden.astype(F32), axis=0, keepdims=True)
    gwe_s[...] += dot_tn(rows, d_hidden)
    e2_ref[...] = dot_nt(d_hidden, we_ref[...]).astype(BF16)

    @pl.when(i == pl.num_programs(0) - 1)
    def _():
        gwe_ref[...] = gwe_s[...].astype(BF16)
        gwr_ref[...] = gwr_s[...].astype(BF16)


def backward_kernel(
    parts, lengths_ref, res_ref, cot_ref, x1_ref, e2_ref, q_ref, mixed_ref, lse_ref, k_ref, v_ref,
    gain_one_ref, gain_ref, w_ref, wo_ref,
    e1_ref, own_ref, tok_ref, gw_ref, gwo_ref, gb_ref, gbo_ref, gg_ref,
    dk_s, dv_s, gw_s, gwo_s,
):
    step = pl.program_id(0)
    i = pl.num_programs(0) - 1 - step
    width = q_ref.shape[1]
    heads = width // HEAD

    @pl.when(step == 0)
    def _():
        for ref in (dk_s, dv_s, gw_s, gwo_s, gb_ref, gbo_ref, gg_ref):
            ref[...] = jnp.zeros_like(ref)

    x1 = x1_ref[...]
    inverse = lax.rsqrt(jnp.mean(x1 * x1, axis=1, keepdims=True) + EPSILON)
    e2 = e2_ref[...].astype(F32)
    gg_ref[...] += jnp.sum(e2 * x1 * inverse, axis=0, keepdims=True)
    c = e2 * gain_ref[...]
    along = jnp.sum(c * x1, axis=1, keepdims=True)
    du = inverse * c - x1 * (inverse * inverse * inverse * along / D)
    g1 = branch_grad(cot_ref[...].astype(F32)) + center(du)
    gbo_ref[...] += jnp.sum(g1, axis=0, keepdims=True)
    g1_last = g1[:, D - 1 :]
    me = lax.axis_index("mp")
    for part in range(parts):

        @pl.when(me == part)
        def _():
            own_ref[...] = g1[:, part * width : (part + 1) * width]

    g1 = g1.astype(BF16)
    mixed = mixed_ref[...]
    gwo_s[...] += dot_tn(mixed, g1)
    d_mixed = dot_nt(g1, wo_ref[...]).astype(BF16)

    product = d_mixed.astype(F32) * mixed.astype(F32)
    product = jnp.transpose(jnp.concatenate([product, jnp.zeros((SHORT, HEAD), F32)], axis=1))
    delta = [
        jnp.sum(product[h * HEAD : (h + 1) * HEAD], axis=0, keepdims=True) for h in range(heads)
    ]
    lse = [lse_ref[h : h + 1] for h in range(heads)]
    is_long, total = flags(lengths_ref)
    live = i * SHORT < total
    far = jnp.where(is_long, 0.0, FAR)
    scaled = q_ref[...] * SCORE_SCALE
    q_heads = [head_of(scaled, h) for h in range(heads)]
    g_heads = [head_of(d_mixed, h) for h in range(heads)]
    q_stack = jnp.concatenate(q_heads, axis=0)
    g_stack = jnp.concatenate(g_heads, axis=0)

    def pair(there, lse, allowed):
        k_j = k_ref[there]
        v_j = v_ref[there]
        probs, scores = [], []
        for h in range(heads):
            p = jnp.exp(dot_nt(k_j, q_heads[h]) - lse[h])
            if allowed is not None:
                p = jnp.where(allowed, p, 0.0)
            probs.append(p.astype(BF16))
            scores.append((p * (dot_nt(v_j, g_heads[h]) - delta[h])).astype(BF16))
        dv_s[there] += dot(jnp.concatenate(probs, axis=1), g_stack)
        dk_s[there] += dot(jnp.concatenate(scores, axis=1), q_stack)
        k_scaled = k_j * SCORE_SCALE
        k_stack = jnp.concatenate([head_of(k_scaled, h) for h in range(heads)], axis=0)
        return dot_tn(jnp.concatenate(scores, axis=0), k_stack)

    here = pl.ds(pl.multiple_of(i * SHORT, SHORT), SHORT)
    dq = pair(here, lse, diagonal(live, True))
    lse_far = [row + far for row in lse]

    def body(j, dq):
        return dq + pair(pl.ds(pl.multiple_of(j * SHORT, SHORT), SHORT), lse_far, None)

    dq = lax.fori_loop(0, i, body, dq).astype(BF16)
    dk = dk_s[here].astype(BF16)
    dv = dv_s[here].astype(BF16)
    gb_ref[0:1] += jnp.sum(dq.astype(F32), axis=0, keepdims=True)
    gb_ref[1:2] += jnp.sum(dv.astype(F32), axis=0, keepdims=True)

    full, inverse = decompress(res_ref[...].astype(F32))
    rows = (full * inverse * gain_one_ref[...]).astype(BF16)
    e1 = jnp.zeros((SHORT, D), F32)
    for n, d in enumerate((dq, dk, dv)):
        gw_s[n] += dot_tn(rows, d)
        e1 = e1 + dot_nt(d, w_ref[n])
    c = e1 * gain_one_ref[...]
    along = jnp.sum(c * full, axis=1, keepdims=True)
    e1_ref[...] = e1.astype(BF16)
    lane = lanes((SHORT, 128))
    tok = jnp.zeros((SHORT, 128), F32)
    for n, column in enumerate((along, c[:, D - 1 :], inverse, full[:, D - 1 :], g1_last)):
        tok = jnp.where(lane == n, column, tok)
    tok_ref[...] = tok

    @pl.when(step == pl.num_programs(0) - 1)
    def _():
        gw_ref[...] = gw_s[...].astype(BF16)
        gwo_ref[...] = gwo_s[...].astype(BF16)


def whole(shape):
    return pl.BlockSpec(shape, lambda i: (0,) * len(shape))


def params(limit=60):
    return pltpu.CompilerParams(vmem_limit_bytes=limit << 20)


def on_device(
    residual,
    lengths,
    gain_one,
    input_weight,
    input_bias,
    output_weight,
    output_bias,
    gain_two,
    expand_weight,
    expand_bias,
    reduce_weight,
    reduce_bias,
    cotangent,
):
    count, width = residual.shape
    parts = D // width
    hidden = expand_weight.shape[1]
    blocks = count // SHORT
    me = lax.axis_index("mp")

    def shape(*dims, dtype=F32):
        return jax.ShapeDtypeStruct(dims, dtype)

    up = lambda w: pl.BlockSpec((SHORT, w), lambda i: (i, 0))
    down = lambda w: pl.BlockSpec((SHORT, w), lambda i: (blocks - 1 - i, 0))
    smem = pl.BlockSpec(memory_space=SMEM)

    def own(vector):
        return lax.dynamic_slice_in_dim(vector, me * width, width, vector.ndim - 1)

    gains = lax.all_gather(
        jnp.stack([gain_one, output_bias, gain_two, reduce_bias]), "mp", axis=1, tiled=True
    )
    res_full = lax.all_gather(residual, "mp", axis=1, tiled=True)
    cot_full = lax.all_gather(cotangent, "mp", axis=1, tiled=True)
    wo_full = lax.all_gather(output_weight, "mp", axis=0, tiled=True)

    q, k, v, mixed, lse = pl.pallas_call(
        forward_kernel,
        grid=(blocks,),
        in_specs=[smem, up(D), whole((1, D)), whole((3, D, width)), whole((2, width))],
        out_specs=[up(width)] * 4 + [pl.BlockSpec((8, SHORT), lambda i: (0, i))],
        out_shape=[shape(count, width, dtype=BF16)] * 4 + [shape(8, count)],
        scratch_shapes=[VMEM((count, width), BF16), VMEM((count, width + HEAD), BF16)],
        compiler_params=params(),
        name="forward",
    )(lengths, res_full, gains[0:1], input_weight, input_bias)

    mixed_full = lax.all_gather(mixed, "mp", axis=1, tiled=True)

    x1, b2, e2, gwe, gwr, gbe, gbr = pl.pallas_call(
        middle_kernel,
        grid=(blocks,),
        in_specs=[up(D)] * 3
        + [whole((D, D)), whole((1, D)), whole((1, D))]
        + [whole((D, hidden)), whole((1, hidden)), whole((hidden, D))],
        out_specs=[up(D)] * 3
        + [whole((D, hidden)), whole((hidden, D)), whole((1, hidden)), whole((1, D))],
        out_shape=[
            shape(count, D),
            shape(count, D, dtype=BF16),
            shape(count, D, dtype=BF16),
            shape(D, hidden, dtype=BF16),
            shape(hidden, D, dtype=BF16),
            shape(1, hidden),
            shape(1, D),
        ],
        scratch_shapes=[VMEM((D, hidden), F32), VMEM((hidden, D), F32)],
        compiler_params=params(),
        name="middle",
    )(
        res_full, cot_full, mixed_full, wo_full, gains[1:2], gains[2:3],
        expand_weight, expand_bias[None], reduce_weight,
    )

    e2 = lax.psum(e2, "mp")
    gwe, gwr = lax.psum((gwe, gwr), "dp")
    b2 = lax.psum_scatter(b2, "mp", scatter_dimension=1, tiled=True)

    e1, g_own, tok, gw, gwo, gb, gbo, gg = pl.pallas_call(
        functools.partial(backward_kernel, parts),
        grid=(blocks,),
        in_specs=[smem, down(D), down(D), down(D), down(D), down(width), down(width)]
        + [pl.BlockSpec((8, SHORT), lambda i: (0, blocks - 1 - i))]
        + [whole((count, width))] * 2
        + [whole((1, D)), whole((1, D)), whole((3, D, width)), whole((width, D))],
        out_specs=[down(D), down(width), down(128)]
        + [whole((3, D, width)), whole((width, D)), whole((2, width)), whole((1, D)), whole((1, D))],
        out_shape=[
            shape(count, D, dtype=BF16),
            shape(count, width),
            shape(count, 128),
            shape(3, D, width, dtype=BF16),
            shape(width, D, dtype=BF16),
            shape(2, width),
            shape(1, D),
            shape(1, D),
        ],
        scratch_shapes=[
            VMEM((count, width), F32),
            VMEM((count, width), F32),
            VMEM((3, D, width), F32),
            VMEM((width, D), F32),
        ],
        compiler_params=params(),
        name="backward",
    )(
        lengths, res_full, cot_full, x1, e2, q, mixed, lse, k, v,
        gains[0:1], gains[2:3], input_weight, output_weight,
    )

    columns = me * width + jnp.arange(width)
    stored = (columns < D - 1)[None, :]
    e1 = lax.psum_scatter(e1, "mp", scatter_dimension=1, tiled=True).astype(F32)
    along, c_last = lax.psum((tok[:, 0], tok[:, 1]), "mp")
    inverse, u_last, g_last = tok[:, 2], tok[:, 3], tok[:, 4]
    u_own = jnp.where(stored, residual.astype(F32), u_last[:, None])
    cube = inverse * inverse * inverse * along / D
    result = g_own + inverse[:, None] * (e1 * gain_one[None]) - u_own * cube[:, None]
    last = g_last + inverse * c_last - u_last * cube
    residual_grad = jnp.where(stored, result - last[:, None], 0.0).astype(BF16)
    gain_one_grad = jnp.sum(e1 * u_own * inverse[:, None], axis=0)

    x2 = own(x1) + b2.astype(F32) + (reduce_bias - jnp.mean(gains[3]))[None]
    residual_out = jnp.where(stored, x2, 0.0).astype(BF16)
    live = jnp.arange(count) < jnp.sum(lengths)
    square = jnp.sum(jnp.where(live[:, None], x2 * x2, 0.0))
    square = lax.psum(square, ("dp", "mp"))
    live_count = lax.psum(jnp.sum(lengths), "dp")
    small = jnp.concatenate(
        [gb.reshape(-1), own(gbo[0]), gain_one_grad, own(gg[0]), gbe[0], own(gbr[0])]
    )
    after = gwe[0, 0] * 0
    gw, gwo = gw + after, gwo + after
    gw, gwo = lax.psum((gw, gwo), "dp")
    small = lax.psum(small, "dp")
    cuts = []
    start = 0
    for size in (2 * width, width, width, width, hidden, width):
        cuts.append(small[start : start + size])
        start += size
    residual_rms = jnp.sqrt(square / (D * live_count.astype(F32)))
    return (
        residual_out,
        residual_grad,
        gw.astype(F32),
        cuts[0].reshape(2, width),
        gwo.astype(F32),
        cuts[1],
        cuts[2],
        cuts[3],
        gwe.astype(F32),
        cuts[4],
        gwr.astype(F32),
        cuts[5],
        residual_rms,
        live_count,
    )


def solution(mesh):
    return jax.shard_map(
        on_device,
        mesh=mesh,
        in_specs=(
            P("dp", "mp"),
            P("dp", None),
            P("mp"),
            P(None, None, "mp"),
            P(None, "mp"),
            P("mp", None),
            P("mp"),
            P("mp"),
            P(None, "mp"),
            P("mp"),
            P("mp", None),
            P("mp"),
            P("dp", "mp"),
        ),
        out_specs=(
            P("dp", "mp"),
            P("dp", "mp"),
            P(None, None, "mp"),
            P(None, "mp"),
            P("mp", None),
            P("mp"),
            P("mp"),
            P("mp"),
            P(None, "mp"),
            P("mp"),
            P("mp", None),
            P("mp"),
            P(),
            P(),
        ),
        check_vma=False,
    )
```

```python
import types

import jax
import jax.numpy as jnp
from jax import lax
from jax.experimental import pallas as pl
from jax.experimental.pallas import tpu as pltpu
from jax.sharding import PartitionSpec as P

D = 768
HEAD = 64
SHORT = 512
HALF = SHORT // 2
LONG = 2048
EPSILON = 1e-05
SCORE_SCALE = 0.125
FAR = 1e30
LANES = 128
MESH = pl.DeviceIdType.MESH

F32 = jnp.float32
BF16 = jnp.bfloat16
NT = (((1,), (1,)), ((), ()))
TN = (((0,), (0,)), ((), ()))


def dot(a, b):
    return jnp.dot(a, b, preferred_element_type=F32)


def dot_nt(a, b):
    return lax.dot_general(a, b, NT, preferred_element_type=F32)


def dot_tn(a, b):
    return lax.dot_general(a, b, TN, preferred_element_type=F32)


def lanes(shape):
    return lax.broadcasted_iota(jnp.int32, shape, 1)


def rows_of(shape):
    return lax.broadcasted_iota(jnp.int32, shape, 0)


def at(index, size):
    return pl.ds(pl.multiple_of(index * size, size), size)


def decompress(raw):
    pad = lanes(raw.shape) == D - 1
    kept = jnp.where(pad, 0.0, raw)
    full = jnp.where(pad, -jnp.sum(kept, axis=1, keepdims=True), kept)
    return full, inverse_rms(full)


def inverse_rms(full):
    return lax.rsqrt(jnp.mean(full * full, axis=1, keepdims=True) + EPSILON)


def center(rows):
    return rows - jnp.mean(rows, axis=1, keepdims=True)


def branch_grad(raw):
    pad = lanes(raw.shape) == D - 1
    return center(jnp.where(pad, 0.0, raw))


def head_of(values, head):
    return jnp.where(lanes(values.shape) // HEAD == head, values, jnp.zeros_like(values))


def diagonal(live, transposed):
    a = rows_of((SHORT, SHORT))
    b = lanes((SHORT, SHORT))
    query, key = (b, a) if transposed else (a, b)
    return (key == query) | ((key < query) & live)


def pack(rows):
    tail = rows[:, LANES:]
    return jnp.concatenate(
        [rows[:, :LANES], jnp.concatenate([tail[:HALF], tail[HALF:]], axis=1)], axis=0
    )


def unpack(piece):
    tail = piece[SHORT:]
    tail = jnp.concatenate([tail[:, : LANES // 2], tail[:, LANES // 2 :]], axis=0)
    return jnp.concatenate([piece[:SHORT], tail], axis=1)


PACKED = SHORT + HALF


def copy_to(src, dst, send_sem, recv_sem, peer):
    return pltpu.make_async_remote_copy(
        src_ref=src,
        dst_ref=dst,
        send_sem=send_sem,
        recv_sem=recv_sem,
        device_id={"mp": peer},
        device_id_type=MESH,
    )


class Gather:
    def __init__(self, piece, sems, me, core, across):
        self.piece, self.me, self.core, self.across = piece, me, core, across
        self.send, self.recv = sems

    def copy(self, kind, i):
        slot = self.across if kind == 2 else self.me
        peer = self.across if kind == 1 else self.core
        here = self.piece(slot, i)
        return copy_to(here, here, self.send.at[kind, i], self.recv.at[kind, i], peer)

    def start(self, i):
        self.copy(1, i).start()
        self.copy(0, i).start()

    def forward(self, i):
        self.copy(1, i).wait_recv()
        self.copy(2, i).start()

    def finish(self, i):
        self.copy(0, i).wait_recv()
        self.copy(2, i).wait_recv()

    def drain(self, i):
        for kind in range(3):
            self.copy(kind, i).wait_send()


INPUTS = ("lengths", "res", "cot", "vec", "w", "bias", "wo", "we", "be", "wr")
OUTPUTS = ("out", "grad", "gw", "gwo", "gwe", "gwr", "small")
IN_HBM = ("res", "cot", "wo", "we", "wr", "out", "grad", "gw", "gwo", "gwe", "gwr")


class Reduce:
    def __init__(self, buf, first, second, other, sems, dp, size):
        self.buf, self.first, self.second, self.other = buf, first, second, other
        self.sems = sems
        self.high = buf.shape[0] // 2
        self.count = size // 2
        self.piece = self.high // self.count
        self.side = lax.rem(dp, 2)
        self.place = lax.div(dp, 2)
        self.mate = dp + 1 - 2 * self.side

    def rows(self, p, base=0):
        return pl.ds(pl.multiple_of(base + p * self.piece, self.piece), self.piece)

    def own(self, p):
        return self.buf.at[self.rows(p, self.side * self.high)]

    def copy(self, src, dst, stage, p, slot, peer):
        return pltpu.make_async_remote_copy(
            src_ref=src,
            dst_ref=dst,
            send_sem=self.sems[0].at[stage, p],
            recv_sem=self.sems[1].at[stage, slot],
            device_id={"dp": peer},
            device_id_type=MESH,
        )

    def to_mate(self, p):
        away = self.buf.at[self.rows(p, (1 - self.side) * self.high)]
        return self.copy(away, self.first.at[self.rows(p)], 0, p, p, self.mate)

    def to_owner(self, p, slot):
        return self.copy(
            self.first.at[self.rows(p)], self.second.at[self.rows(slot)], 1, p, slot, 2 * p + self.side
        )

    def to_peer(self, p, slot):
        return self.copy(self.own(slot), self.own(slot), 2, p, slot, 2 * p + self.side)

    def back(self, p):
        return self.copy(self.own(p), self.other.at[self.rows(p)], 3, p, p, self.mate)

    def each(self, body, start=0, stop=None):
        def run(p, _):
            body(p)
            return 0

        lax.fori_loop(start, self.count if stop is None else stop, run, 0)

    def others(self, body):
        def run(p):
            @pl.when(p != self.place)
            def _():
                body(p)

        self.each(run)

    def start(self):
        self.each(lambda p: self.to_mate(p).start())

    def sum_mates(self, p):
        self.to_mate(p).wait_recv()
        here = self.rows(p)
        both = self.buf[self.rows(p, self.side * self.high)].astype(F32) + self.first[here].astype(F32)
        self.first[here] = both.astype(BF16)

        @pl.when(p != self.place)
        def _():
            self.to_owner(p, self.place).start()

    def sum_quarter(self, q):
        self.each(self.sum_mates, q * self.count // 4, (q + 1) * self.count // 4)

    def sum_owners(self):
        self.second[self.rows(self.place)] = self.first[self.rows(self.place)]
        self.others(lambda q: self.to_owner(q, q).wait_recv())
        total = lax.fori_loop(
            0,
            self.count,
            lambda q, acc: acc + self.second[self.rows(q)].astype(F32),
            jnp.zeros((self.piece, self.buf.shape[1]), F32),
        )
        self.buf[self.rows(self.place, self.side * self.high)] = total.astype(BF16)
        self.others(lambda p: self.to_peer(p, self.place).start())
        self.back(self.place).start()

    def forward(self):
        def body(q):
            self.to_peer(q, q).wait_recv()
            self.back(q).start()

        self.others(body)

    def finish(self):
        self.each(lambda p: self.back(p).wait_recv())

    def take(self, body):
        for side in range(2):

            @pl.when(self.side == side)
            def _(side=side):
                body(side, self.buf.at[side * self.high : (side + 1) * self.high])
                body(1 - side, self.other)

    def drain(self):
        self.each(lambda p: self.to_mate(p).wait_send())
        self.others(lambda p: self.to_owner(p, self.place).wait_send())
        self.others(lambda p: self.to_peer(p, self.place).wait_send())
        self.each(lambda p: self.back(p).wait_send())


def scratch(count, width, hidden, groups):
    parts = D // width
    blocks = count // SHORT
    bf, f = BF16, F32
    arrays = dict(
        RES=((parts, blocks * PACKED, LANES), bf),
        COT=((parts, blocks * PACKED, LANES), bf),
        MIX=((parts, blocks * PACKED, LANES), bf),
        VEC=((parts, 8, 2 * LANES), f),
        GAINS=((8, D), f),
        WO=((D, D), bf),
        Q=((count, width), bf),
        K=((count, width), bf),
        VX=((count, width + HEAD), bf),
        LSE=((blocks, 8, SHORT), f),
        X1=((count, D), f),
        E2P=((count, D), bf),
        E2C=((blocks, HALF, D), bf),
        E2Y=((blocks, HALF, D), bf),
        E2T=((blocks, HALF, D), bf),
        PIECES=((2, parts, PACKED, LANES), bf),
        B2C=((2, blocks, PACKED, LANES), bf),
        B2Y=((blocks, PACKED, LANES), bf),
        E1C=((2, blocks, PACKED, LANES), bf),
        E1Y=((blocks, PACKED, LANES), bf),
        STAT=((parts, blocks, 8, SHORT), f),
        DV=((3 * D, width), f),
        GWE=((3 * D, 2 * LANES), f),
        GWR=((3 * D, 2 * LANES), f),
        ACC=((8, D), f),
        BM=((2 * D, hidden), bf),
        BM1=((D, hidden), bf),
        BM2=((D, hidden), bf),
        BM3=((D, hidden), bf),
        BT=((2 * D, 2 * width), bf),
        WE=((D, hidden), bf),
        WR=((hidden, D), bf),
        SMALL=((groups, 16, 2 * LANES), f),
        GB=((8, width), f),
    )
    sems = dict(
        load=(1, 5), store=(1, 8), bm=(4, groups // 2), bt=(4, groups // 2), tiny=(1, groups),
        res=(3, blocks), cot=(3, blocks), mix=(3, blocks), wo_=(3, 1), vec_=(3, 1),
        e2a=(1, blocks), e2x=(1, blocks), e2b=(1, blocks),
        b2c=(2, blocks), b2x=(1, blocks), e1c=(2, blocks), e1x=(1, blocks), stat=(3, blocks),
    )
    names, shapes = [], []
    for name, (shape, dtype) in arrays.items():
        names.append(name)
        shapes.append(pltpu.VMEM(shape, dtype))
    for name, shape in sems.items():
        for way in ("s", "r"):
            names.append(f"{name}_{way}")
            shapes.append(pltpu.SemaphoreType.DMA(shape))
    return names, shapes


def layer_kernel(groups, names, *refs):
    n = types.SimpleNamespace(**dict(zip((*INPUTS, *OUTPUTS, *names), refs, strict=True)))
    count, width = n.res.shape
    parts = D // width
    blocks = count // SHORT
    heads = width // HEAD
    hidden = n.we.shape[1]
    me = lax.axis_index("mp")
    core = me + 1 - 2 * lax.rem(me, 2)
    across = lax.rem(me + parts // 2, parts)
    corner = lax.rem(core + parts // 2, parts)
    side = lax.rem(me, 2)
    peers = (core, across, corner)
    dp = lax.axis_index("dp")

    loads = [
        pltpu.make_async_copy(src, dst, n.load_s.at[0, k])
        for k, (src, dst) in enumerate(
            ((n.res, n.Q), (n.cot, n.K), (n.wo, n.WO.at[at(me, width)]), (n.we, n.WE), (n.wr, n.WR))
        )
    ]
    for c in loads:
        c.start()
    barrier = pltpu.get_barrier_semaphore()
    for peer in peers:
        pl.semaphore_signal(barrier, inc=1, device_id={"mp": peer}, device_id_type=MESH)

    def each_group(body):
        def run(d, _):
            body(d, lax.rem(dp + d, groups))
            return 0

        lax.fori_loop(1, groups, run, 0)

    each_group(
        lambda d, group: pl.semaphore_signal(
            barrier, inc=1, device_id={"dp": group}, device_id_type=MESH
        )
    )
    pl.semaphore_wait(barrier, len(peers) + groups - 1)
    feed = Reduce(n.BM, n.BM1, n.BM2, n.BM3, (n.bm_s, n.bm_r), dp, groups)
    spare = (n.WE.at[:, : 2 * width], n.WE.at[:, 2 * width :], n.WR.at[:, : 2 * width])
    rest = Reduce(n.BT, *spare, (n.bt_s, n.bt_r), dp, groups)

    def gather(buf, sems):
        return Gather(
            lambda slot, i: buf.at[slot, at(i, PACKED)], sems, me, core, across
        )

    res = gather(n.RES, (n.res_s, n.res_r))
    cot = gather(n.COT, (n.cot_s, n.cot_r))
    mix = gather(n.MIX, (n.mix_s, n.mix_r))
    weight = Gather(lambda slot, i: n.WO.at[at(slot, width)], (n.wo__s, n.wo__r), me, core, across)

    def vec_copy(k):
        return copy_to(n.VEC.at[me], n.VEC.at[me], n.vec__s.at[k, 0], n.vec__r.at[k, 0], peers[k])

    def join(buf, i):
        pieces = [unpack(buf[p, at(i, PACKED)]) for p in range(parts)]
        return jnp.concatenate(pieces, axis=1)

    def own_columns(ref_write, values):
        for p in range(parts):

            @pl.when(me == p)
            def _():
                ref_write(values[:, p * width : (p + 1) * width])

    n.VEC[me] = n.vec[...]
    for k in range(3):
        vec_copy(k).start()
    for c in loads[:1]:
        c.wait()
    for i in range(blocks):
        n.RES[me, i * PACKED : (i + 1) * PACKED] = pack(n.Q[i * SHORT : (i + 1) * SHORT])
        res.start(i)
    for c in loads[1:]:
        c.wait()
    for i in range(blocks):
        n.COT[me, i * PACKED : (i + 1) * PACKED] = pack(n.K[i * SHORT : (i + 1) * SHORT])
    for ref in (n.GWE, n.GWR, n.DV, n.ACC, n.GB):
        ref[...] = jnp.zeros_like(ref)
    total = n.lengths[0, 0]
    for slot in range(1, n.lengths.shape[1]):
        total = total + n.lengths[0, slot]
    far = jnp.where(n.lengths[0, 0] == LONG, 0.0, FAR)
    for k in range(3):
        vec_copy(k).wait_recv()
    for row in range(4):
        n.GAINS[row : row + 1] = jnp.concatenate(
            [n.VEC[p, row : row + 1, :width] for p in range(parts)], axis=1
        )

    def forward_block(i, _):
        res.forward(i)

        @pl.when(i == 1)
        def _():
            weight.start(0)

        @pl.when(i >= 2)
        def _():
            cot.start(2 * i - 4)
            cot.start(2 * i - 3)

        res.finish(i)
        here = at(i, SHORT)
        full, inverse = decompress(join(n.RES, i).astype(F32))
        rows = (full * inverse * n.GAINS[0:1]).astype(BF16)
        q = (dot(rows, n.w[0]) + n.bias[0:1]).astype(BF16)
        k = dot(rows, n.w[1]).astype(BF16)
        v = (dot(rows, n.w[2]) + n.bias[1:2]).astype(BF16)
        v = jnp.concatenate([v, jnp.ones((SHORT, HEAD), BF16)], axis=1)
        n.Q[here] = q
        n.K[here] = k
        n.VX[here] = v
        live = i * SHORT < total
        allowed = diagonal(live, False)
        scaled = q * SCORE_SCALE
        q_heads = [head_of(scaled, h) for h in range(heads)]
        carry = []
        for h in range(heads):
            s = jnp.where(allowed, dot_nt(q_heads[h], k), -FAR)
            m = jnp.max(s, axis=1, keepdims=True)
            carry.append((m, dot(jnp.exp(s - m).astype(BF16), v)))

        def body(j, carry):
            k_j = n.K[at(j, SHORT)]
            v_j = n.VX[at(j, SHORT)]
            after = []
            for h in range(heads):
                m, acc = carry[h]
                s = dot_nt(q_heads[h], k_j)
                new = jnp.maximum(m, jnp.max(s, axis=1, keepdims=True) - far)
                p = jnp.exp(s - (new + far)).astype(BF16)
                after.append((new, acc * jnp.exp(m - new) + dot(p, v_j)))
            return after

        carry = lax.fori_loop(0, i, body, carry)
        mixed = jnp.zeros((SHORT, width), F32)
        lse = jnp.zeros((SHORT, LANES), F32)
        for h in range(heads):
            m, acc = carry[h]
            norm = acc[:, width : width + 1]
            mixed = mixed + head_of(acc[:, :width] / norm, h)
            lse = jnp.where(lanes(lse.shape) == h, m + jnp.log(norm), lse)
        n.LSE[i] = jnp.transpose(lse)[:8]
        n.MIX[me, at(i, PACKED)] = pack(mixed.astype(BF16))
        mix.start(i)

        @pl.when(i >= 1)
        def _():
            mix.forward(i - 1)

        return 0

    lax.fori_loop(0, blocks, forward_block, 0)

    def e2_half(i, which):
        return n.E2P.at[pl.ds(pl.multiple_of(i * SHORT + which * HALF, HALF), HALF)]

    def e2_first(i):
        return copy_to(e2_half(i, 1 - side), n.E2C.at[i], n.e2a_s.at[0, i], n.e2a_r.at[0, i], core)

    def e2_cross(i):
        return copy_to(n.E2C.at[i], n.E2Y.at[i], n.e2x_s.at[0, i], n.e2x_r.at[0, i], across)

    def e2_last(i):
        return copy_to(e2_half(i, side), n.E2T.at[i], n.e2b_s.at[0, i], n.e2b_r.at[0, i], core)

    def e2_sum(i):
        e2_first(i).wait_recv()
        own = n.E2P[pl.ds(pl.multiple_of(i * SHORT + side * HALF, HALF), HALF)].astype(F32)
        n.E2C[i] = (own + n.E2C[i].astype(F32)).astype(BF16)
        e2_cross(i).start()

    def e2_total(i):
        e2_cross(i).wait_recv()
        both = n.E2C[i].astype(F32) + n.E2Y[i].astype(F32)
        n.E2P[pl.ds(pl.multiple_of(i * SHORT + side * HALF, HALF), HALF)] = both.astype(BF16)
        e2_last(i).start()

    def scatter_first(P, C, sems, slot, i):
        targets = (core, corner)
        return [
            copy_to(P.at[slot, targets[k]], C.at[k, i], sems[0].at[k, i], sems[1].at[k, i], core)
            for k in range(2)
        ]

    def scatter_sum(P, C, first, slot, i):
        for c in first:
            c.wait_recv()
        for k, owner in enumerate((me, across)):
            C[k, i] = (P[slot, owner].astype(F32) + C[k, i].astype(F32)).astype(BF16)

    def scatter_cross(C, Y, sems, i):
        return copy_to(C.at[1, i], Y.at[i], sems[0].at[0, i], sems[1].at[0, i], across)

    b2_sems, b2x_sems = (n.b2c_s, n.b2c_r), (n.b2x_s, n.b2x_r)
    e1_sems, e1x_sems = (n.e1c_s, n.e1c_r), (n.e1x_s, n.e1x_r)

    def b2_first(slot, i):
        return scatter_first(n.PIECES, n.B2C, b2_sems, slot, i)

    def b2_cross(i):
        return scatter_cross(n.B2C, n.B2Y, b2x_sems, i)

    def e1_first(slot, i):
        return scatter_first(n.PIECES, n.E1C, e1_sems, slot, i)

    def e1_cross(i):
        return scatter_cross(n.E1C, n.E1Y, e1x_sems, i)

    def split(P, slot, values):
        for p in range(parts):
            P[slot, p] = pack(values[:, p * width : (p + 1) * width])

    def order(step):
        return lax.rem(blocks - step, blocks)

    weight.forward(0)
    cot.forward(0)
    cot.forward(1)
    weight.finish(0)

    def add_thirds(ref, values):
        for c in range(3):
            ref[c * D : (c + 1) * D] += values[:, c * 2 * LANES : (c + 1) * 2 * LANES]

    def middle_block(step, _):
        i = order(step)
        slot = lax.rem(step, 2)

        @pl.when(step == 1)
        def _():
            mix.forward(blocks - 1)
            cot.forward(2)
            cot.forward(3)

        mix.finish(i)
        cot.finish(i)
        here = at(i, SHORT)
        full, _unused = decompress(join(n.RES, i).astype(F32))
        x1 = full + center(dot(join(n.MIX, i), n.WO[...]) + n.GAINS[1:2])
        n.X1[here] = x1
        rows = (x1 * inverse_rms(x1) * n.GAINS[2:3]).astype(BF16)
        z = dot(rows, n.WE[...]) + n.be[...]
        t = jnp.tanh(0.7978845608 * (z + 0.044715 * (z * z * z)))
        active = (0.5 * z * (1.0 + t)).astype(BF16)
        slope = 0.5 * (1.0 + t) + 0.5 * z * (1.0 - t * t) * (
            0.7978845608 * (1.0 + (3 * 0.044715) * (z * z))
        )
        slope = slope.astype(BF16)

        @pl.when(step >= 2)
        def _():
            e2_sum(order(step - 1))

        @pl.when(step >= 1)
        def _():
            before = order(step - 1)
            scatter_sum(n.PIECES, n.B2C, b2_first(1 - slot, before), 1 - slot, before)

        @pl.when(step >= 2)
        def _():
            for c in b2_first(slot, order(step - 2)):
                c.wait_send()

        split(n.PIECES, slot, center(dot(active, n.WR[...])).astype(BF16))
        for c in b2_first(slot, i):
            c.start()
        g2 = branch_grad(join(n.COT, i).astype(F32))
        n.ACC[0:1] += jnp.sum(g2, axis=0, keepdims=True)
        g2 = g2.astype(BF16)
        add_thirds(n.GWR, dot_tn(active, g2))
        d_hidden = (dot_nt(g2, n.WR[...]) * slope).astype(BF16)
        n.ACC[1:2, :hidden] += jnp.sum(d_hidden.astype(F32), axis=0, keepdims=True)
        add_thirds(n.GWE, dot_tn(rows, d_hidden))
        n.E2P[here] = dot_nt(d_hidden, n.WE[...]).astype(BF16)
        e2_first(i).start()
        return 0

    lax.fori_loop(0, blocks, middle_block, 0)
    last = (blocks - 1) % 2
    e2_sum(order(blocks - 1))
    e2_sum(0)
    scatter_sum(n.PIECES, n.B2C, b2_first(last, order(blocks - 1)), last, order(blocks - 1))
    for c in range(3):
        block = slice(c * 2 * LANES, (c + 1) * 2 * LANES)
        n.BM[:D, block] = n.GWE[c * D : (c + 1) * D].astype(BF16)
        n.BM[D:, block] = n.GWR[c * D : (c + 1) * D].astype(BF16)
    feed.start()

    for slot, step in ((1 - last, blocks - 2), (last, blocks - 1)):
        for c in b2_first(slot, order(step)):
            c.wait_send()
    n.GWE[...] = jnp.zeros_like(n.GWE)
    n.GWR[...] = jnp.zeros_like(n.GWR)

    x1_own, tokens = 2 * LANES, 4 * LANES

    def stat_copy(k, i):
        mine = n.STAT.at[me, i]
        return copy_to(mine, mine, n.stat_s.at[k, i], n.stat_r.at[k, i], peers[k])

    columns = me * width + lanes((1, width))
    stored = columns < D - 1

    def finish_grad(i):
        here = at(i, SHORT)
        e1_cross(i).wait_recv()
        for k in range(3):
            stat_copy(k, i).wait_recv()
        stat = jnp.zeros((8, SHORT), F32)
        for p in range(parts):
            stat = stat + n.STAT[p, i]
        stat = jnp.transpose(jnp.concatenate([stat] * (LANES // 8), axis=0))
        along, c_last = stat[:, 0:1], stat[:, 1:2]

        @pl.when(i == 0)
        def _():
            n.GB[4:5] = jnp.zeros((1, width), F32) + jnp.sum(
                sum(n.STAT[p, i, 2:3] for p in range(parts)), axis=1, keepdims=True
            )

        tok = n.X1[here, tokens : tokens + LANES]
        inverse, u_last, g_last = tok[:, 0:1], tok[:, 1:2], tok[:, 2:3]
        e1 = unpack(n.E1C[0, i].astype(F32) + n.E1Y[i].astype(F32))
        u_own = jnp.where(stored, unpack(n.RES[me, at(i, PACKED)]).astype(F32), u_last)
        n.GB[2:3] += jnp.sum(e1 * u_own * inverse, axis=0, keepdims=True)
        cube = inverse * inverse * inverse * along / D
        own = n.X1[here, :width] + inverse * (e1 * n.vec[0:1, :width]) - u_own * cube
        final = g_last + inverse * c_last - u_last * cube
        n.Q[here] = jnp.where(stored, own - final, 0.0).astype(BF16)

    def finish_out(i):
        here = at(i, SHORT)
        b2_cross(i).wait_recv()
        b2 = unpack(n.B2C[0, i].astype(F32) + n.B2Y[i].astype(F32))
        bias = n.vec[3:4, :width] - jnp.mean(n.GAINS[3:4], axis=1, keepdims=True)
        live = (i * SHORT + rows_of((SHORT, 1))) < total

        x2 = n.X1[here, x1_own : x1_own + width] + b2 + bias
        n.K[here] = jnp.where(stored, x2, 0.0).astype(BF16)
        n.GB[3:4] += jnp.sum(jnp.where(live, x2 * x2, 0.0), axis=0, keepdims=True)

    def backward_block(step, _):
        i = blocks - 1 - step
        slot = lax.rem(step, 2)
        here = at(i, SHORT)

        @pl.when(step == 0)
        def _():
            e2_total(i)

        @pl.when(step == 1)
        def _():
            for b in range(blocks):
                b2_cross(b).start()

        e2_last(i).wait_recv()
        e2_first(i).wait_send()
        n.E2P[pl.ds(pl.multiple_of(i * SHORT + (1 - side) * HALF, HALF), HALF)] = n.E2T[i]
        x1 = n.X1[here]
        inverse = inverse_rms(x1)
        e2 = n.E2P[here].astype(F32)
        n.ACC[2:3] += jnp.sum(e2 * x1 * inverse, axis=0, keepdims=True)
        c = e2 * n.GAINS[2:3]
        along = jnp.sum(c * x1, axis=1, keepdims=True)
        du = inverse * c - x1 * (inverse * inverse * inverse * along / D)
        g1 = branch_grad(join(n.COT, i).astype(F32)) + center(du)
        n.ACC[3:4] += jnp.sum(g1, axis=0, keepdims=True)
        g1_last = g1[:, D - 1 :]

        for p in range(parts):

            @pl.when(me == p)
            def _():
                n.X1[here, :width] = g1[:, p * width : (p + 1) * width]
                n.X1[here, x1_own : x1_own + width] = x1[:, p * width : (p + 1) * width]

        g1 = g1.astype(BF16)
        mixed = unpack(n.MIX[me, at(i, PACKED)])
        g_output = dot_tn(g1, mixed)
        for h in range(heads):
            n.GWE[h * D : (h + 1) * D, width:] += g_output[:, h * HEAD : (h + 1) * HEAD]
        d_mixed = dot_nt(g1, n.WO[at(me, width)]).astype(BF16)
        product = d_mixed.astype(F32) * mixed.astype(F32)
        product = jnp.transpose(jnp.concatenate([product, jnp.zeros((SHORT, HEAD), F32)], axis=1))
        delta = [
            jnp.sum(product[h * HEAD : (h + 1) * HEAD], axis=0, keepdims=True)
            for h in range(heads)
        ]
        lse = [n.LSE[i, h : h + 1] for h in range(heads)]
        live = i * SHORT < total
        scaled = n.Q[here] * SCORE_SCALE
        q_heads = [head_of(scaled, h) for h in range(heads)]
        g_heads = [head_of(d_mixed, h) for h in range(heads)]
        def pair(there, lse, allowed):
            k_j = n.K[there]
            v_j = n.VX[there][:, :width]
            k_scaled = k_j * SCORE_SCALE
            dk = dv = dq = jnp.zeros((SHORT, width), F32)
            for h in range(heads):
                p = jnp.exp(dot_nt(k_j, q_heads[h]) - lse[h])
                if allowed is not None:
                    p = jnp.where(allowed, p, 0.0)
                dv = dv + dot(p.astype(BF16), g_heads[h])
                p = (p * (dot_nt(v_j, g_heads[h]) - delta[h])).astype(BF16)
                dk = dk + dot(p, q_heads[h])
                dq = dq + dot_tn(p, head_of(k_scaled, h))
            n.DV[there] += dv
            n.GWR[there, :width] += dk
            return dq

        dq = pair(here, lse, diagonal(live, True))

        @pl.when(i >= 1)
        def _():
            e2_total(i - 1)

        @pl.when(step == 1)
        def _():
            feed.sum_quarter(3)

        @pl.when(step == 2)
        def _():
            feed.sum_owners()

        @pl.when(step == blocks - 1)
        def _():
            for b in range(blocks):
                finish_out(b)

        @pl.when(step >= 1)
        def _():
            scatter_sum(n.PIECES, n.E1C, e1_first(1 - slot, i + 1), 1 - slot, i + 1)
            e1_cross(i + 1).start()

        lse_far = [row + far for row in lse]

        def body(j, dq):
            dq = dq + pair(at(j, SHORT), lse_far, None)

            @pl.when(step == 0)
            def _():
                feed.sum_quarter(j)

            return dq

        dq = lax.fori_loop(0, i, body, dq).astype(BF16)
        dk = n.GWR[here, :width].astype(BF16)
        dv = n.DV[here].astype(BF16)
        n.GB[0:1] += jnp.sum(dq.astype(F32), axis=0, keepdims=True)
        n.GB[1:2] += jnp.sum(dv.astype(F32), axis=0, keepdims=True)
        full, inverse = decompress(join(n.RES, i).astype(F32))
        rows = (full * inverse * n.GAINS[0:1]).astype(BF16)
        e1 = jnp.zeros((SHORT, D), F32)
        for c, d in enumerate((dq, dk, dv)):
            n.GWE[c * D : (c + 1) * D, :width] += dot_tn(rows, d)
            e1 = e1 + dot_nt(d, n.w[c])

        @pl.when(step >= 2)
        def _():
            for c in e1_first(slot, i + 2):
                c.wait_send()

        split(n.PIECES, slot, e1.astype(BF16))
        for c in e1_first(slot, i):
            c.start()
        c = e1 * n.GAINS[0:1]
        lane = lanes((SHORT, LANES))
        stat = jnp.where(lane == 0, jnp.sum(c * full, axis=1, keepdims=True), 0.0)
        stat = jnp.where(lane == 1, c[:, D - 1 :], stat)
        n.STAT[me, i] = jnp.transpose(stat)[:8]
        n.STAT[me, i, 2:3, :width] = n.GB[3:4]
        for k in range(3):
            stat_copy(k, i).start()
        tok = jnp.where(lane == 0, inverse, 0.0)
        tok = jnp.where(lane == 1, full[:, D - 1 :], tok)
        n.X1[here, tokens : tokens + LANES] = jnp.where(lane == 2, g1_last, tok)

        @pl.when(step >= 2)
        def _():
            finish_grad(i + 2)

        return 0

    lax.fori_loop(0, blocks, backward_block, 0)
    scatter_sum(n.PIECES, n.E1C, e1_first(last, 0), last, 0)
    e1_cross(0).start()

    for c in range(3):
        n.BT[c // 2 * D : c // 2 * D + D, c % 2 * width : c % 2 * width + width] = n.GWE[
            c * D : (c + 1) * D, :width
        ].astype(BF16)
    n.BT[D:, width:] = jnp.concatenate(
        [n.GWE[h * D : (h + 1) * D, width:] for h in range(heads)], axis=1
    ).astype(BF16)
    rest.start()
    finish_grad(1)
    feed.forward()
    rest.sum_quarter(0)
    rest.sum_quarter(1)
    finish_grad(0)
    rest.sum_quarter(2)
    rest.sum_quarter(3)

    def tiny_copy(slot, group):
        here = n.SMALL.at[dp]
        return pltpu.make_async_remote_copy(
            src_ref=here,
            dst_ref=here,
            send_sem=n.tiny_s.at[0, group],
            recv_sem=n.tiny_r.at[0, slot],
            device_id={"dp": group},
            device_id_type=MESH,
        )

    n.SMALL[dp] = jnp.zeros((16, 2 * LANES), F32)
    n.SMALL[dp, 0:3, :width] = n.GB[0:3]
    n.SMALL[dp, 3:4, :width] = n.GB[4:5]
    n.SMALL[dp, 7:8] = jnp.zeros((1, 2 * LANES), F32) + total.astype(F32)
    for row, source in ((4, 3), (5, 2), (6, 0)):

        def write_small(values, row=row):
            n.SMALL[dp, row : row + 1, :width] = values

        own_columns(write_small, n.ACC[source : source + 1])
    for p in range(parts):
        n.SMALL[dp, 8 + p : 9 + p, :width] = n.ACC[1:2, p * width : (p + 1) * width]
    each_group(lambda d, group: tiny_copy(dp, group).start())

    def store(src, dst, k):
        return pltpu.make_async_copy(src, dst, n.store_s.at[0, k])

    stores = [store(n.Q, n.grad, 0), store(n.K, n.out, 1)]
    for c in stores:
        c.start()
    rest.sum_owners()
    feed.finish()

    def store_feed(half, rows):
        target, k = ((n.gwe, 2), (n.gwr, 3))[half]
        stage = n.X1.at[half * D : (half + 1) * D]
        stage[...] = rows[...].astype(F32)
        store(stage, target, k).start()

    feed.take(store_feed)
    stores += [store(n.X1.at[:D], n.gwe, 2), store(n.X1.at[D : 2 * D], n.gwr, 3)]
    rest.forward()
    each_group(lambda d, group: tiny_copy(group, group).wait_recv())
    small = n.SMALL[0]
    for group in range(1, groups):
        small = small + n.SMALL[group]
    n.small[...] = small
    rest.finish()

    def store_rest(half, rows):
        if half == 0:
            n.DV[:D] = rows[:, :width].astype(F32)
            n.DV[D : 2 * D] = rows[:, width:].astype(F32)
            store(n.DV.at[:D], n.gw.at[0], 4).start()
            store(n.DV.at[D : 2 * D], n.gw.at[1], 5).start()
        else:
            n.DV[2 * D :] = rows[:, :width].astype(F32)
            store(n.DV.at[2 * D :], n.gw.at[2], 6).start()
            n.X1[2 * D : 2 * D + width] = jnp.transpose(rows[:, width:].astype(F32))
            store(n.X1.at[2 * D : 2 * D + width], n.gwo, 7).start()

    rest.take(store_rest)
    stores += [
        store(n.DV.at[:D], n.gw.at[0], 4),
        store(n.DV.at[D : 2 * D], n.gw.at[1], 5),
        store(n.DV.at[2 * D :], n.gw.at[2], 6),
        store(n.X1.at[2 * D : 2 * D + width], n.gwo, 7),
    ]

    for k in range(3):
        vec_copy(k).wait_send()
    weight.drain(0)

    def drain(i, _):
        for g in (res, cot, mix):
            g.drain(i)
        for c in (e2_cross, e2_last, b2_cross, e1_cross):
            c(i).wait_send()
        for k in range(3):
            stat_copy(k, i).wait_send()
        return 0

    lax.fori_loop(0, blocks, drain, 0)
    for step in (blocks - 2, blocks - 1):
        for c in e1_first(step % 2, blocks - 1 - step):
            c.wait_send()
    for c in stores:
        c.wait()
    feed.drain()
    rest.drain()
    each_group(lambda d, group: tiny_copy(dp, group).wait_send())


def on_device(
    residual,
    lengths,
    gain_one,
    input_weight,
    input_bias,
    output_weight,
    output_bias,
    gain_two,
    expand_weight,
    expand_bias,
    reduce_weight,
    reduce_bias,
    cotangent,
):
    count, width = residual.shape
    hidden = expand_weight.shape[1]

    def shape(*dims, dtype=BF16):
        return jax.ShapeDtypeStruct(dims, dtype)

    vec = jnp.stack([gain_one, output_bias, gain_two, reduce_bias])
    vec = jnp.pad(vec, ((0, 4), (0, 2 * LANES - width)))
    groups = lax.axis_size("dp")
    names, scratches = scratch(count, width, hidden, groups)
    vmem = pl.BlockSpec(memory_space=pltpu.VMEM)
    hbm = pl.BlockSpec(memory_space=pl.ANY)
    out, grad, gw, gwo, gwe, gwr, small = pl.pallas_call(
        lambda *refs: layer_kernel(groups, names, *refs),
        in_specs=[pl.BlockSpec(memory_space=pltpu.SMEM)]
        + [hbm if name in IN_HBM else vmem for name in INPUTS[1:]],
        out_specs=[hbm if name in IN_HBM else vmem for name in OUTPUTS],
        out_shape=[
            shape(count, width),
            shape(count, width),
            shape(3, D, width, dtype=F32),
            shape(width, D, dtype=F32),
            shape(D, hidden, dtype=F32),
            shape(hidden, D, dtype=F32),
            shape(16, 2 * LANES, dtype=F32),
        ],
        scratch_shapes=scratches,
        compiler_params=pltpu.CompilerParams(
            vmem_limit_bytes=63 << 20, collective_id=0, has_side_effects=True
        ),
        name="layer",
    )(
        lengths, residual, cotangent, vec, input_weight, input_bias, output_weight,
        expand_weight, expand_bias[None], reduce_weight,
    )

    small = small[:, :width]
    live_count = small[7, 0].astype(jnp.int32)
    residual_rms = jnp.sqrt(small[3, 0] / (D * small[7, 0]))
    return (
        out,
        grad,
        gw,
        small[0:2],
        gwo,
        small[4],
        small[2],
        small[5],
        gwe,
        small[8:12].reshape(hidden),
        gwr,
        small[6],
        residual_rms,
        live_count,
    )


def solution(mesh):
    return jax.shard_map(
        on_device,
        mesh=mesh,
        in_specs=(
            P("dp", "mp"),
            P("dp", None),
            P("mp"),
            P(None, None, "mp"),
            P(None, "mp"),
            P("mp", None),
            P("mp"),
            P("mp"),
            P(None, "mp"),
            P("mp"),
            P("mp", None),
            P("mp"),
            P("dp", "mp"),
        ),
        out_specs=(
            P("dp", "mp"),
            P("dp", "mp"),
            P(None, None, "mp"),
            P(None, "mp"),
            P("mp", None),
            P("mp"),
            P("mp"),
            P("mp"),
            P(None, "mp"),
            P("mp"),
            P("mp", None),
            P("mp"),
            P(),
            P(),
        ),
        check_vma=False,
    )
```

```python
import types

import jax
import jax.numpy as jnp
from jax import lax
from jax.experimental import pallas as pl
from jax.experimental.pallas import tpu as pltpu
from jax.sharding import PartitionSpec as P


D = 768
HEAD = 64
SHORT = 512
LONG = 2048
EPSILON = 1e-05
SCORE_SCALE = 0.125
FAR = 1e30
LANES = 128
SUBLANES = 8
MESH = pl.DeviceIdType.MESH

F32 = jnp.float32
BF16 = jnp.bfloat16
NT = (((1,), (1,)), ((), ()))


def dot(a, b):
    return jnp.dot(a, b, preferred_element_type=F32)


def dot_nt(a, b):
    return lax.dot_general(a, b, NT, preferred_element_type=F32)


def lanes(shape):
    return lax.broadcasted_iota(jnp.int32, shape, 1)


def rows_of(shape):
    return lax.broadcasted_iota(jnp.int32, shape, 0)


def at(index, size):
    return pl.ds(pl.multiple_of(index * size, size), size)


def column_sum(values):
    return jnp.sum(values, axis=0, keepdims=True)


def with_last(values, last):
    cut = values.shape[0] - SUBLANES
    end = values[cut:]
    end = jnp.where(rows_of(end.shape) == SUBLANES - 1, last, end)
    return jnp.concatenate([values[:cut], end], axis=0)


def decompress(raw):
    full = with_last(raw, 0.0)
    full = with_last(full, -column_sum(full))
    return full, inverse_rms(full)


def inverse_rms(full):
    return lax.rsqrt(column_sum(full * full) / D + EPSILON)


def center(values):
    return values - column_sum(values) / D


def branch_grad(raw):
    return center(with_last(raw, 0.0))


def diagonal(live):
    key = rows_of((SHORT, SHORT))
    query = lanes((SHORT, SHORT))
    return (key == query) | ((key < query) & live)


def pick(lane):
    return (lanes((SHORT, LANES)) == lane).astype(BF16)


def copy_to(src, dst, send_sem, recv_sem, peer):
    return pltpu.make_async_remote_copy(
        src_ref=src,
        dst_ref=dst,
        send_sem=send_sem,
        recv_sem=recv_sem,
        device_id={"mp": peer},
        device_id_type=MESH,
    )


class Gather:
    def __init__(self, piece, source, sems, me, core, across):
        self.piece, self.source = piece, source
        self.me, self.core, self.across = me, core, across
        self.send, self.recv = sems

    def copy(self, kind, i):
        slot = self.across if kind == 2 else self.me
        peer = self.across if kind == 1 else self.core
        there = self.piece(slot, i)
        here = there if kind == 2 else self.source(i)
        return copy_to(here, there, self.send.at[kind, i], self.recv.at[kind, i], peer)

    def start(self, i):
        self.copy(1, i).start()
        self.copy(0, i).start()

    def forward(self, i):
        self.copy(1, i).wait_recv()
        self.copy(2, i).start()

    def finish(self, i):
        self.copy(0, i).wait_recv()
        self.copy(2, i).wait_recv()

    def drain(self, i):
        for kind in range(3):
            self.copy(kind, i).wait_send()


INPUTS = ("lengths", "res", "cot", "vec", "w", "wo", "we", "wr")
OUTPUTS = ("out", "grad", "rest", "feed", "small")
IN_VMEM = ("vec", "small")


class Reduce:
    def __init__(self, buf, first, second, other, sems, dp, size):
        self.buf, self.first, self.second, self.other = buf, first, second, other
        self.sems = sems
        self.high = buf.shape[0] // 2
        self.count = size // 2
        self.piece = self.high // self.count
        self.side = lax.rem(dp, 2)
        self.place = lax.div(dp, 2)
        self.mate = dp + 1 - 2 * self.side

    def rows(self, p, base=0):
        return pl.ds(pl.multiple_of(base + p * self.piece, self.piece), self.piece)

    def own(self, p):
        return self.buf.at[self.rows(p, self.side * self.high)]

    def copy(self, src, dst, stage, p, slot, peer):
        return pltpu.make_async_remote_copy(
            src_ref=src,
            dst_ref=dst,
            send_sem=self.sems[0].at[stage, p],
            recv_sem=self.sems[1].at[stage, slot],
            device_id={"dp": peer},
            device_id_type=MESH,
        )

    def to_mate(self, p):
        away = self.buf.at[self.rows(p, (1 - self.side) * self.high)]
        return self.copy(away, self.first.at[self.rows(p)], 0, p, p, self.mate)

    def to_owner(self, p, slot):
        return self.copy(
            self.first.at[self.rows(p)], self.second.at[self.rows(slot)], 1, p, slot, 2 * p + self.side
        )

    def to_peer(self, p, slot):
        return self.copy(self.own(slot), self.own(slot), 2, p, slot, 2 * p + self.side)

    def back(self, p):
        return self.copy(self.own(p), self.other.at[self.rows(p)], 3, p, p, self.mate)

    def each(self, body, start=0, stop=None):
        def run(p, _):
            body(p)
            return 0

        lax.fori_loop(start, self.count if stop is None else stop, run, 0)

    def others(self, body):
        def run(p):
            @pl.when(p != self.place)
            def _():
                body(p)

        self.each(run)

    def turn(self, k):
        half = self.count // 2
        return lax.rem(k, 2) * half + lax.div(k, 2)

    def start(self):
        self.each(lambda k: self.to_mate(self.turn(k)).start())

    def sum_mates(self, p):
        self.to_mate(p).wait_recv()
        here = self.rows(p)
        both = self.buf[self.rows(p, self.side * self.high)].astype(F32) + self.first[here].astype(F32)
        self.first[here] = both.astype(BF16)

        @pl.when(p != self.place)
        def _():
            self.to_owner(p, self.place).start()

    def sum_quarter(self, q):
        self.each(
            lambda k: self.sum_mates(self.turn(k)), q * self.count // 4, (q + 1) * self.count // 4
        )

    def sum_owners(self):
        self.second[self.rows(self.place)] = self.first[self.rows(self.place)]
        self.others(lambda q: self.to_owner(q, q).wait_recv())
        total = lax.fori_loop(
            0,
            self.count,
            lambda q, acc: acc + self.second[self.rows(q)].astype(F32),
            jnp.zeros((self.piece, self.buf.shape[1]), F32),
        )
        self.buf[self.rows(self.place, self.side * self.high)] = total.astype(BF16)
        self.others(lambda p: self.to_peer(p, self.place).start())
        self.back(self.place).start()

    def forward(self):
        def body(q):
            self.to_peer(q, q).wait_recv()
            self.back(q).start()

        self.others(body)

    def finish(self):
        self.each(lambda p: self.back(p).wait_recv())

    def take(self, body):
        for side in range(2):

            @pl.when(self.side == side)
            def _(side=side):
                body(side, self.buf.at[side * self.high : (side + 1) * self.high])
                body(1 - side, self.other)

    def drain(self):
        self.each(lambda p: self.to_mate(p).wait_send())
        self.others(lambda p: self.to_owner(p, self.place).wait_send())
        self.others(lambda p: self.to_peer(p, self.place).wait_send())
        self.each(lambda p: self.back(p).wait_send())


def scratch(count, width, hidden, groups):
    parts = D // width
    blocks = count // SHORT
    bf, f = BF16, F32
    arrays = dict(
        RES=((D, count), bf),
        COT=((D, count), bf),
        MIX=((D, count), bf),
        VEC=((parts, SUBLANES, 2 * LANES), f),
        COLS=((D, LANES), f),
        WO=((D, D), bf),
        WE=((D, hidden), bf),
        WET=((hidden, D), bf),
        WR=((hidden, D), bf),
        WN=((D, 3 * width), bf),
        QT=((width, count), bf),
        KT=((width, count), bf),
        VT=((width, count), bf),
        KN=((count, width), bf),
        VN=((count, width), bf),
        LSE=((blocks, SUBLANES, SHORT), f),
        TOK=((blocks, SUBLANES, SHORT), f),
        X1=((D, count), f),
        E2P=((D, count), bf),
        E2C=((blocks, D // 2, SHORT), bf),
        E2Y=((blocks, D // 2, SHORT), bf),
        E2T=((blocks, D // 2, SHORT), bf),
        PIECES=((2, parts, width, SHORT), bf),
        B2C=((2, blocks, width, SHORT), bf),
        B2Y=((blocks, width, SHORT), bf),
        E1C=((2, blocks, width, SHORT), bf),
        E1Y=((blocks, width, SHORT), bf),
        STAT=((parts, blocks, SUBLANES, SHORT), f),
        GWE=((D, hidden), f),
        GWR=((hidden, D), f),
        GW=((3 * width + width, D), f),
        ACC=((D, LANES), f),
        OWN=((3 * width, LANES), f),
        SQ=((parts, SUBLANES, SHORT), f),
        BM=((2 * D, hidden), bf),
        BM1=((D, hidden), bf),
        BM2=((D, hidden), bf),
        BT=((2 * D, 2 * width), bf),
        SMALL=((groups, 16, 2 * LANES), f),
    )
    sems = dict(
        load=(1, 8), store=(1, 8), bm=(4, groups // 2), bt=(4, groups // 2), tiny=(1, groups),
        res=(3, blocks), cot=(3, blocks), mix=(3, blocks), wo_=(3, 1), vec_=(3, 1), sq=(3, 1),
        e2a=(1, blocks), e2x=(1, blocks), e2b=(1, blocks),
        b2c=(2, blocks), b2x=(1, blocks), e1c=(2, blocks), e1x=(1, blocks), stat=(3, blocks),
    )
    names, shapes = [], []
    for name, (shape, dtype) in arrays.items():
        names.append(name)
        shapes.append(pltpu.VMEM(shape, dtype))
    for name, shape in sems.items():
        for way in ("s", "r"):
            names.append(f"{name}_{way}")
            shapes.append(pltpu.SemaphoreType.DMA(shape))
    return names, shapes


def layer_kernel(groups, names, *refs):
    n = types.SimpleNamespace(**dict(zip((*INPUTS, *OUTPUTS, *names), refs, strict=True)))
    width, count = n.res.shape
    parts = D // width
    blocks = count // SHORT
    heads = width // HEAD
    hidden = n.we.shape[1]
    me = lax.axis_index("mp")
    core = me + 1 - 2 * lax.rem(me, 2)
    across = lax.rem(me + parts // 2, parts)
    corner = lax.rem(core + parts // 2, parts)
    side = lax.rem(me, 2)
    peers = (core, across, corner)
    dp = lax.axis_index("dp")
    own = at(me, width)

    def tokens(i):
        return at(i, SHORT)

    loads = [
        pltpu.make_async_copy(src, dst, n.load_s.at[0, k])
        for k, (src, dst) in enumerate(
            (
                (n.w, n.BM.at[: 3 * width]),
                (n.wo, n.WO.at[own]),
                (n.res, n.RES.at[own]),
                (n.we, n.WE),
                (n.wr, n.WR),
                (n.cot, n.COT.at[own]),
            )
        )
    ]
    barrier = pltpu.get_barrier_semaphore()
    for peer in peers:
        pl.semaphore_signal(barrier, inc=1, device_id={"mp": peer}, device_id_type=MESH)

    def each_group(body):
        def run(d, _):
            body(d, lax.rem(dp + d, groups))
            return 0

        lax.fori_loop(1, groups, run, 0)

    each_group(
        lambda d, group: pl.semaphore_signal(
            barrier, inc=1, device_id={"dp": group}, device_id_type=MESH
        )
    )
    for c in loads:
        c.start()
    pl.semaphore_wait(barrier, len(peers) + groups - 1)

    feed = Reduce(n.BM, n.BM1, n.BM2, n.WET, (n.bm_s, n.bm_r), dp, groups)
    spare = (n.WE.at[:, : 2 * width], n.WE.at[:, 2 * width :], n.WR.at[:, : 2 * width])
    rest = Reduce(n.BT, *spare, (n.bt_s, n.bt_r), dp, groups)

    def gather(buf, source, sems):
        return Gather(
            lambda slot, i: buf.at[at(slot, width), tokens(i)],
            lambda i: source.at[:, tokens(i)],
            sems, me, core, across,
        )

    res = gather(n.RES, n.res, (n.res_s, n.res_r))
    cot = gather(n.COT, n.cot, (n.cot_s, n.cot_r))
    mix = gather(n.MIX, n.MIX.at[own], (n.mix_s, n.mix_r))
    weight = Gather(
        lambda slot, i: n.WO.at[at(slot, width)],
        lambda i: n.wo,
        (n.wo__s, n.wo__r), me, core, across,
    )

    def vec_copy(k):
        return copy_to(n.vec.at[:SUBLANES], n.VEC.at[me], n.vec__s.at[k, 0], n.vec__r.at[k, 0], peers[k])

    res.start(0)
    for k in range(3):
        vec_copy(k).start()
    for i in range(1, blocks):
        res.start(i)
    n.VEC[me] = n.vec[:SUBLANES]
    loads[0].wait()
    n.WN[...] = jnp.transpose(n.BM[: 3 * width])
    for ref in (n.GWE, n.GWR, n.GW, n.ACC, n.OWN, n.SQ):
        ref[...] = jnp.zeros_like(ref)
    total = n.lengths[0, 0]
    for slot in range(1, n.lengths.shape[1]):
        total = total + n.lengths[0, slot]
    far = jnp.where(n.lengths[0, 0] == LONG, 0.0, FAR)
    for c in loads[1:5]:
        c.wait()
    n.WET[...] = jnp.transpose(n.WE[...])
    for k in range(2):
        n.BT[k * D : (k + 1) * D] = jnp.transpose(n.WR[k * 2 * width : (k + 1) * 2 * width])
    for k in range(3):
        vec_copy(k).wait_recv()
    vectors = jnp.concatenate([n.VEC[p][:, :width] for p in range(parts)], axis=1)
    be = jnp.concatenate(
        [n.vec[SUBLANES + p : SUBLANES + p + 1, :width] for p in range(parts)], axis=1
    )
    vectors = jnp.where(rows_of(vectors.shape) == 6, be, vectors)
    vectors = jnp.concatenate([vectors, jnp.zeros((LANES - SUBLANES, D), F32)], axis=0)
    n.COLS[...] = jnp.transpose(vectors)
    loads[5].wait()

    def col(k):
        return n.COLS[:, k : k + 1]

    def own_col(k):
        return n.COLS[own, k : k + 1]

    def halves(values):
        pair = values[: 2 * HEAD]
        row = rows_of(pair.shape)
        zero = jnp.zeros_like(pair)
        return (jnp.where(row < HEAD, pair, zero), jnp.where(row < HEAD, zero, pair), values[2 * HEAD :])

    def part_of(values, h):
        return values[:, : 2 * HEAD] if h < 2 else values[:, 2 * HEAD :]

    def head_rows(values, h):
        return values[h * HEAD : (h + 1) * HEAD]

    def forward_block(i, _):
        res.forward(i)

        @pl.when(i == 2)
        def _():
            weight.start(0)
            cot.start(0)

        res.finish(i)
        here = tokens(i)
        full, inverse = decompress(n.RES[:, here].astype(F32))
        rows = (full * inverse * col(0)).astype(BF16)
        qkv = dot(n.BM[: 3 * width], rows)
        q = (qkv[:width] + own_col(4)).astype(BF16)
        k = qkv[width : 2 * width].astype(BF16)
        v = (qkv[2 * width :] + own_col(5)).astype(BF16)
        k_rows = jnp.transpose(k)
        n.QT[:, here] = q
        n.KT[:, here] = k
        n.VT[:, here] = v
        n.KN[here] = k_rows
        n.VN[here] = jnp.transpose(v)
        live = i * SHORT < total
        allowed = diagonal(live)
        q_heads = halves(q * SCORE_SCALE)
        carry = []
        for h in range(heads):
            s = jnp.where(allowed, dot(part_of(k_rows, h), q_heads[h]), -FAR)
            m = jnp.max(s, axis=0, keepdims=True)
            p = jnp.exp(s - m)
            carry.append((m, column_sum(p), dot(head_rows(v, h), p.astype(BF16))))

        def body(j, carry):
            k_j = n.KN[tokens(j)]
            v_j = n.VT[:, tokens(j)]
            after = []
            for h in range(heads):
                m, norm, acc = carry[h]
                s = dot(part_of(k_j, h), q_heads[h])
                new = jnp.maximum(m, jnp.max(s, axis=0, keepdims=True) - far)
                p = jnp.exp(s - (new + far))
                scale = jnp.exp(m - new)
                after.append(
                    (new, norm * scale + column_sum(p), acc * scale + dot(head_rows(v_j, h), p.astype(BF16)))
                )
            return after

        carry = lax.fori_loop(0, i, body, carry)
        mixed = []
        for h in range(heads):
            m, norm, acc = carry[h]
            mixed.append(acc / norm)
            n.LSE[i, h : h + 1] = m + jnp.log(norm)
        n.MIX[own, here] = jnp.concatenate(mixed, axis=0).astype(BF16)

        @pl.when(i == 0)
        def _():
            mix.start(i)

        return 0

    lax.fori_loop(0, blocks, forward_block, 0)

    high = D // 2

    def e2_half(i, which):
        return n.E2P.at[at(which, high), tokens(i)]

    def e2_first(i):
        return copy_to(e2_half(i, 1 - side), n.E2C.at[i], n.e2a_s.at[0, i], n.e2a_r.at[0, i], core)

    def e2_cross(i):
        return copy_to(n.E2C.at[i], n.E2Y.at[i], n.e2x_s.at[0, i], n.e2x_r.at[0, i], across)

    def e2_last(i):
        return copy_to(e2_half(i, side), n.E2T.at[i], n.e2b_s.at[0, i], n.e2b_r.at[0, i], core)

    def e2_sum(i):
        e2_first(i).wait_recv()
        mine = n.E2P[at(side, high), tokens(i)].astype(F32)
        n.E2C[i] = (mine + n.E2C[i].astype(F32)).astype(BF16)
        e2_cross(i).start()

    def e2_total(i):
        e2_cross(i).wait_recv()
        both = n.E2C[i].astype(F32) + n.E2Y[i].astype(F32)
        n.E2P[at(side, high), tokens(i)] = both.astype(BF16)
        e2_last(i).start()

    def scatter_first(C, sems, slot, i):
        targets = (core, corner)
        return [
            copy_to(
                n.PIECES.at[slot, targets[k]], C.at[k, i], sems[0].at[k, i], sems[1].at[k, i], core
            )
            for k in range(2)
        ]

    def scatter_sum(C, first, slot, i):
        for c in first:
            c.wait_recv()
        for k, owner in enumerate((me, across)):
            C[k, i] = (n.PIECES[slot, owner].astype(F32) + C[k, i].astype(F32)).astype(BF16)

    def scatter_cross(C, Y, sems, i):
        return copy_to(C.at[1, i], Y.at[i], sems[0].at[0, i], sems[1].at[0, i], across)

    def b2_first(slot, i):
        return scatter_first(n.B2C, (n.b2c_s, n.b2c_r), slot, i)

    def b2_cross(i):
        return scatter_cross(n.B2C, n.B2Y, (n.b2x_s, n.b2x_r), i)

    def e1_first(slot, i):
        return scatter_first(n.E1C, (n.e1c_s, n.e1c_r), slot, i)

    def e1_cross(i):
        return scatter_cross(n.E1C, n.E1Y, (n.e1x_s, n.e1x_r), i)

    def split(slot, values):
        for p in range(parts):
            n.PIECES[slot, p] = values[p * width : (p + 1) * width]

    def order(step):
        return lax.rem(blocks - step, blocks)

    for i in range(blocks - 1, 0, -1):
        mix.start(i)
        cot.start(i)
    mix.forward(0)
    weight.forward(0)
    cot.forward(0)
    weight.finish(0)
    n.BM[D:] = jnp.transpose(n.WO[...])

    def middle_block(step, _):
        i = order(step)
        slot = lax.rem(step, 2)

        @pl.when(step >= 1)
        def _():
            mix.forward(i)
            cot.forward(i)

        mix.finish(i)
        cot.finish(i)
        here = tokens(i)
        full, _unused = decompress(n.RES[:, here].astype(F32))
        x1 = full + center(dot(n.BM[D:], n.MIX[:, here]) + col(1))
        n.X1[:, here] = x1
        rows = (x1 * inverse_rms(x1) * col(2)).astype(BF16)
        z = dot(n.WET[...], rows) + col(6)
        square = z * z
        h = 0.5 + 0.5 * jnp.tanh(z * (0.7978845608 + (0.7978845608 * 0.044715) * square))
        active = z * h
        slope = h + active * (1.0 - h) * (
            2 * 0.7978845608 + (6 * 0.7978845608 * 0.044715) * square
        )
        active = active.astype(BF16)
        slope = slope.astype(BF16)

        @pl.when(step >= 2)
        def _():
            e2_sum(order(step - 1))
            for c in b2_first(slot, order(step - 2)):
                c.wait_send()

        @pl.when(step >= 1)
        def _():
            before = order(step - 1)
            scatter_sum(n.B2C, b2_first(1 - slot, before), 1 - slot, before)

        b2 = dot(n.BT[:D], active[: 2 * width]) + dot(n.BT[D:], active[2 * width :])
        split(slot, center(b2).astype(BF16))
        for c in b2_first(slot, i):
            c.start()
        g2 = branch_grad(n.COT[:, here].astype(F32)).astype(BF16)
        n.GWR[...] += dot_nt(active, g2)
        d_hidden = (dot(n.WR[...], g2) * slope).astype(BF16)
        n.ACC[...] += dot(g2, pick(0)) + dot(d_hidden, pick(1))
        n.GWE[...] += dot_nt(rows, d_hidden)
        n.E2P[:, here] = dot(n.WE[...], d_hidden).astype(BF16)
        e2_first(i).start()
        return 0

    lax.fori_loop(0, blocks, middle_block, 0)
    last = (blocks - 1) % 2
    e2_sum(order(blocks - 1))
    e2_sum(0)
    scatter_sum(n.B2C, b2_first(last, order(blocks - 1)), last, order(blocks - 1))
    n.BM[:D] = n.GWE[...].astype(BF16)
    n.BM[D:] = n.GWR[...].astype(BF16)
    feed.start()
    for slot, step in ((1 - last, blocks - 2), (last, blocks - 1)):
        for c in b2_first(slot, order(step)):
            c.wait_send()
    n.GWE[...] = jnp.zeros_like(n.GWE)
    n.GWR[...] = jnp.zeros_like(n.GWR)

    def stat_copy(k, i):
        mine = n.STAT.at[me, i]
        return copy_to(mine, mine, n.stat_s.at[k, i], n.stat_r.at[k, i], peers[k])

    stored = rows_of((width, 1)) + me * width < D - 1

    def finish_grad(i):
        here = tokens(i)
        e1_cross(i).wait_recv()
        for k in range(3):
            stat_copy(k, i).wait_recv()
        stat = n.STAT[0, i]
        for p in range(1, parts):
            stat = stat + n.STAT[p, i]
        along, c_last = stat[0:1], stat[1:2]
        inverse, u_last, g_last = n.TOK[i, 0:1], n.TOK[i, 1:2], n.TOK[i, 2:3]
        e1 = n.E1C[0, i].astype(F32) + n.E1Y[i].astype(F32)
        u_own = jnp.where(stored, n.RES[own, here].astype(F32), u_last)
        normed = e1 * u_own * inverse
        n.OWN[:width] += dot(normed.astype(BF16), pick(3))
        cube = inverse * inverse * inverse * along / D
        result = n.X1[at(across, width), here] + inverse * (e1 * own_col(0)) - u_own * cube
        final = g_last + inverse * c_last - u_last * cube
        n.QT[:, here] = jnp.where(stored, result - final, 0.0).astype(BF16)

    def finish_out(i):
        here = tokens(i)
        b2_cross(i).wait_recv()
        b2 = n.B2C[0, i].astype(F32) + n.B2Y[i].astype(F32)
        x2 = n.X1[own, here] + b2 + (own_col(3) - jnp.mean(col(3), axis=0, keepdims=True))
        n.VT[:, here] = jnp.where(stored, x2, 0.0).astype(BF16)
        live = lanes((1, SHORT)) + i * SHORT < total
        n.SQ[me, 0:1] += jnp.where(live, column_sum(x2 * x2), 0.0)

    def backward_block(step, _):
        i = blocks - 1 - step
        slot = lax.rem(step, 2)
        here = tokens(i)

        @pl.when(step == 0)
        def _():
            e2_total(i)

        @pl.when(step == 1)
        def _():
            for b in range(blocks):
                b2_cross(b).start()

        e2_last(i).wait_recv()
        e2_first(i).wait_send()
        n.E2P[at(1 - side, high), here] = n.E2T[i]
        x1 = n.X1[:, here]
        inverse = inverse_rms(x1)
        e2 = n.E2P[:, here].astype(F32)
        normed = e2 * x1
        gain_part = (normed * inverse).astype(BF16)
        along = column_sum(normed * col(2))
        du = inverse * (e2 * col(2)) - x1 * (inverse * inverse * inverse * along / D)
        g1 = branch_grad(n.COT[:, here].astype(F32)) + center(du)
        n.TOK[i, 2:3] = g1[D - 1 :]
        for p in range(parts):

            @pl.when(me == p)
            def _():
                n.X1[at(across, width), here] = g1[p * width : (p + 1) * width]

        g1 = g1.astype(BF16)
        n.ACC[...] += dot(gain_part, pick(2)) + dot(g1, pick(3))
        mixed = n.MIX[own, here]
        n.GW[3 * width :] += dot_nt(mixed, g1)
        d_mixed = dot(n.WO[own], g1).astype(BF16)
        product = d_mixed.astype(F32) * mixed.astype(F32)
        delta = [column_sum(head_rows(product, h)) for h in range(heads)]
        lse = [n.LSE[i, h : h + 1] for h in range(heads)]
        live = i * SHORT < total
        q = n.QT[:, here] * SCORE_SCALE
        q_heads = halves(q)
        g_heads = halves(d_mixed)

        def pair(j, lse, allowed):
            there = tokens(j)
            k_j, v_j, k_t = n.KN[there], n.VN[there], n.KT[:, there]
            dq, dk, dv = [], [], []
            for h in range(heads):
                p = jnp.exp(dot(part_of(k_j, h), q_heads[h]) - lse[h])
                if allowed is not None:
                    p = jnp.where(allowed, p, 0.0)
                dv.append(dot_nt(head_rows(d_mixed, h), p.astype(BF16)))
                p = (p * (dot(part_of(v_j, h), g_heads[h]) - delta[h])).astype(BF16)
                dk.append(dot_nt(head_rows(q, h), p))
                dq.append(dot(head_rows(k_t, h), p))
            n.GWE[at(j, width), :SHORT] += jnp.concatenate(dv, axis=0)
            n.GWR[at(j, width), :SHORT] += jnp.concatenate(dk, axis=0)
            return jnp.concatenate(dq, axis=0)

        dq = pair(i, lse, diagonal(live))

        @pl.when(i >= 1)
        def _():
            e2_total(i - 1)

        @pl.when(step == 1)
        def _():
            feed.sum_quarter(2)

        @pl.when(step == blocks - 1)
        def _():
            feed.sum_owners()

        @pl.when(step >= 1)
        def _():
            scatter_sum(n.E1C, e1_first(1 - slot, i + 1), 1 - slot, i + 1)
            e1_cross(i + 1).start()

        lse_far = [row + far for row in lse]

        def body(j, dq):
            dq = dq + pair(j, lse_far, None)

            @pl.when((step == 0) & (j != 1))
            def _():
                feed.sum_quarter(lax.div(j, 2))

            @pl.when((step == 1) & (j == 0))
            def _():
                feed.sum_quarter(3)

            return dq

        dq = lax.fori_loop(0, i, body, dq)
        d_all = jnp.concatenate(
            [dq * SCORE_SCALE, n.GWR[at(i, width), :SHORT], n.GWE[at(i, width), :SHORT]], axis=0
        ).astype(BF16)
        n.OWN[...] += dot(d_all, pick(0))
        full, inverse = decompress(n.RES[:, here].astype(F32))
        rows = (full * inverse * col(0)).astype(BF16)
        n.GW[: 3 * width] += dot_nt(d_all, rows)
        e1 = dot(n.WN[...], d_all)

        @pl.when(step >= 2)
        def _():
            for c in e1_first(slot, i + 2):
                c.wait_send()

        split(slot, e1.astype(BF16))
        for c in e1_first(slot, i):
            c.start()
        c = e1 * col(0)
        n.STAT[me, i, 0:1] = column_sum(c * full)
        n.STAT[me, i, 1:2] = c[D - 1 :]
        for k in range(3):
            stat_copy(k, i).start()
        n.TOK[i, 0:1] = inverse
        n.TOK[i, 1:2] = full[D - 1 :]
        return 0

    lax.fori_loop(0, blocks, backward_block, 0)
    scatter_sum(n.E1C, e1_first(last, 0), last, 0)
    e1_cross(0).start()
    n.BT[:D] = n.GW[:, : 2 * width].astype(BF16)
    n.BT[D:] = n.GW[:, 2 * width :].astype(BF16)
    rest.start()

    def square_copy(k):
        return copy_to(n.SQ.at[me], n.SQ.at[me], n.sq_s.at[k, 0], n.sq_r.at[k, 0], peers[k])

    def finish_block(k, _):
        finish_out(k)
        rest.sum_quarter(k)
        return 0

    lax.fori_loop(0, blocks, finish_block, 0)
    for k in range(3):
        square_copy(k).start()

    def finish_rows(k, _):
        finish_grad(blocks - 1 - k)
        return 0

    feed.forward()
    lax.fori_loop(0, blocks, finish_rows, 0)
    for k in range(3):
        square_copy(k).wait_recv()

    def tiny_copy(slot, group):
        here = n.SMALL.at[dp]
        return pltpu.make_async_remote_copy(
            src_ref=here,
            dst_ref=here,
            send_sem=n.tiny_s.at[0, group],
            recv_sem=n.tiny_r.at[0, slot],
            device_id={"dp": group},
            device_id_type=MESH,
        )

    squares = jnp.sum(sum(n.SQ[p, 0:1] for p in range(parts)), axis=1, keepdims=True)
    mine = n.ACC[own]
    parts_in = [
        n.OWN[:width, 0:1],
        n.OWN[2 * width :, 0:1],
        n.OWN[:width, 3:4],
        squares,
        mine[:, 3:4],
        mine[:, 2:3],
        mine[:, 0:1],
        total.astype(F32),
    ] + [n.ACC[p * width : (p + 1) * width, 1:2] for p in range(parts)]
    table = jnp.zeros((width, LANES), F32)
    for lane, values in enumerate(parts_in):
        table = jnp.where(lanes(table.shape) == lane, values, table)
    table = jnp.concatenate([table, jnp.zeros((2 * LANES - width, LANES), F32)], axis=0)
    n.SMALL[dp] = jnp.transpose(table)[:16]
    each_group(lambda d, group: tiny_copy(dp, group).start())

    def store(src, dst, k):
        return pltpu.make_async_copy(src, dst, n.store_s.at[0, k])

    stores = [store(n.QT, n.grad, 0), store(n.VT, n.out, 1)]
    for c in stores:
        c.start()
    rest.sum_owners()
    each_group(lambda d, group: tiny_copy(group, group).wait_recv())
    small = n.SMALL[0]
    for group in range(1, groups):
        small = small + n.SMALL[group]
    n.small[...] = small
    feed.finish()

    def store_half(target, k):
        def body(half, rows):
            store(rows, target.at[half * D : (half + 1) * D], k + half).start()

        return body

    feed.take(store_half(n.feed, 2))
    rest.forward()
    rest.finish()
    rest.take(store_half(n.rest, 4))
    for k, (buf, target) in enumerate(((n.BM, n.feed), (n.BT, n.rest))):
        for half in range(2):
            here = slice(half * D, (half + 1) * D)
            stores.append(store(buf.at[here], target.at[here], 2 + 2 * k + half))

    for k in range(3):
        vec_copy(k).wait_send()
        square_copy(k).wait_send()
    weight.drain(0)

    def drain(i, _):
        for g in (res, cot, mix):
            g.drain(i)
        for c in (e2_cross, e2_last, b2_cross, e1_cross):
            c(i).wait_send()
        for k in range(3):
            stat_copy(k, i).wait_send()
        return 0

    lax.fori_loop(0, blocks, drain, 0)
    for step in (blocks - 2, blocks - 1):
        for c in e1_first(step % 2, blocks - 1 - step):
            c.wait_send()
    for c in stores:
        c.wait()
    feed.drain()
    rest.drain()
    each_group(lambda d, group: tiny_copy(dp, group).wait_send())


def finish_kernel(
    out, grad, rest_low, rest_high, feed_low, feed_high, small,
    out_ref, grad_ref, gw_ref, gwo_ref, gwe_ref, gwr_ref,
    gb_ref, gbo_ref, gg_one_ref, gg_two_ref, gbe_ref, gbr_ref, rms_ref, live_ref,
):
    i = pl.program_id(0)
    width = gb_ref.shape[1]
    out_ref[...] = out[...]
    grad_ref[...] = grad[...]
    rest = jnp.concatenate([rest_low[...], rest_high[...]], axis=1).astype(F32)
    gwe_ref[...] = feed_low[...].astype(F32)
    gwr_ref[...] = feed_high[...].astype(F32)

    @pl.when(i < 3)
    def _():
        gw_ref[...] = rest

    @pl.when(i == 3)
    def _():
        gwo_ref[...] = rest

    @pl.when(i == 0)
    def _():
        gb_ref[...] = small[0:2, :width]
        gg_one_ref[...] = small[2:3, :width]
        gbo_ref[...] = small[4:5, :width]
        gg_two_ref[...] = small[5:6, :width]
        gbr_ref[...] = small[6:7, :width]
        gbe_ref[...] = jnp.concatenate(
            [small[8 + p : 9 + p, :width] for p in range(D // width)], axis=1
        )
        live = small[7:8, 0:1]
        rms_ref[...] = jnp.sqrt(small[3:4, 0:1] / (D * live))
        live_ref[...] = live.astype(jnp.int32)


def on_device(
    residual,
    lengths,
    gain_one,
    input_weight,
    input_bias,
    output_weight,
    output_bias,
    gain_two,
    expand_weight,
    expand_bias,
    reduce_weight,
    reduce_bias,
    cotangent,
):
    count, width = residual.shape
    hidden = expand_weight.shape[1]
    parts = D // width

    def shape(*dims, dtype=F32):
        return jax.ShapeDtypeStruct(dims, dtype)

    zero = jnp.zeros((2, width), F32)
    vec = jnp.concatenate(
        [gain_one[None], output_bias[None], gain_two[None], reduce_bias[None], input_bias, zero]
        + [expand_bias.reshape(parts, width), zero, zero]
    )
    vec = jnp.pad(vec, ((0, 0), (0, 2 * LANES - width)))
    groups = lax.axis_size("dp")
    names, scratches = scratch(count, width, hidden, groups)

    def space(name):
        return pl.BlockSpec(memory_space=pltpu.VMEM if name in IN_VMEM else pl.ANY)

    out, grad, rest, feed, small = pl.pallas_call(
        lambda *refs: layer_kernel(groups, names, *refs),
        in_specs=[pl.BlockSpec(memory_space=pltpu.SMEM)] + [space(name) for name in INPUTS[1:]],
        out_specs=[space(name) for name in OUTPUTS],
        out_shape=[
            shape(width, count, dtype=BF16),
            shape(width, count, dtype=BF16),
            shape(2 * D, 2 * width, dtype=BF16),
            shape(2 * D, hidden, dtype=BF16),
            shape(16, 2 * LANES),
        ],
        scratch_shapes=scratches,
        compiler_params=pltpu.CompilerParams(
            vmem_limit_bytes=63 << 20, collective_id=0, has_side_effects=True
        ),
        name="layer",
    )(
        lengths,
        residual.T,
        cotangent.T,
        vec,
        jnp.transpose(input_weight, (0, 2, 1)).reshape(3 * width, D),
        output_weight,
        expand_weight,
        reduce_weight,
    )

    def rows(high, wide, base=0):
        return pl.BlockSpec((high, wide), lambda i: (i + base, 0))

    def whole(*dims):
        return pl.BlockSpec(dims, lambda i: (0,) * len(dims))

    def clip(high, wide, first, last):
        return pl.BlockSpec((high, wide), lambda i: (jnp.clip(i - first, 0, last - first), 0))

    step = D // parts
    thin = width // parts
    out, grad, gw, gwo, gwe, gwr, *vectors = pl.pallas_call(
        finish_kernel,
        grid=(parts,),
        in_specs=[
            rows(thin, count),
            rows(thin, count),
            rows(step, 2 * width),
            rows(step, 2 * width, parts),
            rows(step, hidden),
            rows(step, hidden, parts),
            whole(16, 2 * LANES),
        ],
        out_specs=[
            rows(thin, count),
            rows(thin, count),
            clip(width, D, 0, 2),
            clip(width, D, 3, 3),
            rows(step, hidden),
            rows(step, hidden),
            whole(2, width),
            whole(1, width),
            whole(1, width),
            whole(1, width),
            whole(1, hidden),
            whole(1, width),
            whole(1, 1),
            whole(1, 1),
        ],
        out_shape=[
            shape(width, count, dtype=BF16),
            shape(width, count, dtype=BF16),
            shape(3 * width, D),
            shape(width, D),
            shape(D, hidden),
            shape(hidden, D),
            shape(2, width),
            shape(1, width),
            shape(1, width),
            shape(1, width),
            shape(1, hidden),
            shape(1, width),
            shape(1, 1),
            shape(1, 1, dtype=jnp.int32),
        ],
        compiler_params=pltpu.CompilerParams(vmem_limit_bytes=60 << 20),
        name="finish",
    )(out, grad, rest, rest, feed, feed, small)
    gb, gbo, gg_one, gg_two, gbe, gbr, rms, live_count = vectors
    return (
        out.T,
        grad.T,
        jnp.transpose(gw.reshape(3, width, D), (0, 2, 1)),
        gb,
        gwo,
        gbo[0],
        gg_one[0],
        gg_two[0],
        gwe,
        gbe[0],
        gwr,
        gbr[0],
        rms[0, 0],
        live_count[0, 0],
    )


def solution(mesh):
    return jax.shard_map(
        on_device,
        mesh=mesh,
        in_specs=(
            P("dp", "mp"),
            P("dp", None),
            P("mp"),
            P(None, None, "mp"),
            P(None, "mp"),
            P("mp", None),
            P("mp"),
            P("mp"),
            P(None, "mp"),
            P("mp"),
            P("mp", None),
            P("mp"),
            P("dp", "mp"),
        ),
        out_specs=(
            P("dp", "mp"),
            P("dp", "mp"),
            P(None, None, "mp"),
            P(None, "mp"),
            P("mp", None),
            P("mp"),
            P("mp"),
            P("mp"),
            P(None, "mp"),
            P("mp"),
            P("mp", None),
            P("mp"),
            P(),
            P(),
        ),
        check_vma=False,
    )
```

```python
import types

import jax
import jax.numpy as jnp
from jax import lax
from jax.experimental import pallas as pl
from jax.experimental.pallas import tpu as pltpu
from jax.sharding import PartitionSpec as P


D = 768
HEAD = 64
SHORT = 512
LONG = 2048
EPSILON = 1e-05
SCORE_SCALE = 0.125
FAR = 1e30
LANES = 128
SUBLANES = 8
MESH = pl.DeviceIdType.MESH

F32 = jnp.float32
BF16 = jnp.bfloat16
NT = (((1,), (1,)), ((), ()))


def dot(a, b):
    return jnp.dot(a, b, preferred_element_type=F32)


def dot_nt(a, b):
    return lax.dot_general(a, b, NT, preferred_element_type=F32)


def lanes(shape):
    return lax.broadcasted_iota(jnp.int32, shape, 1)


def rows_of(shape):
    return lax.broadcasted_iota(jnp.int32, shape, 0)


def at(index, size):
    return pl.ds(pl.multiple_of(index * size, size), size)


def column_sum(values):
    return jnp.sum(values, axis=0, keepdims=True)


def with_last(values, last):
    cut = values.shape[0] - SUBLANES
    end = values[cut:]
    end = jnp.where(rows_of(end.shape) == SUBLANES - 1, last, end)
    return jnp.concatenate([values[:cut], end], axis=0)


def decompress(raw):
    full = with_last(raw, 0.0)
    full = with_last(full, -column_sum(full))
    return full, inverse_rms(full)


def inverse_rms(full):
    return lax.rsqrt(column_sum(full * full) / D + EPSILON)


def center(values):
    return values - column_sum(values) / D


def branch_grad(raw):
    return center(with_last(raw, 0.0))


def diagonal(live):
    key = rows_of((SHORT, SHORT))
    query = lanes((SHORT, SHORT))
    return (key == query) | ((key < query) & live)


def pick(lane):
    return (lanes((SHORT, LANES)) == lane).astype(BF16)


def copy_to(src, dst, send_sem, recv_sem, peer):
    return pltpu.make_async_remote_copy(
        src_ref=src,
        dst_ref=dst,
        send_sem=send_sem,
        recv_sem=recv_sem,
        device_id={"mp": peer},
        device_id_type=MESH,
    )


class Gather:
    def __init__(self, piece, source, sems, me, core, across):
        self.piece, self.source = piece, source
        self.me, self.core, self.across = me, core, across
        self.send, self.recv = sems

    def copy(self, kind, i):
        slot = self.across if kind == 2 else self.me
        peer = self.across if kind == 1 else self.core
        there = self.piece(slot, i)
        here = there if kind == 2 else self.source(i)
        return copy_to(here, there, self.send.at[kind, i], self.recv.at[kind, i], peer)

    def start(self, i):
        self.copy(1, i).start()
        self.copy(0, i).start()

    def forward(self, i):
        self.copy(1, i).wait_recv()
        self.copy(2, i).start()

    def finish(self, i):
        self.copy(0, i).wait_recv()
        self.copy(2, i).wait_recv()

    def drain(self, i):
        for kind in range(3):
            self.copy(kind, i).wait_send()


class WeightGather:
    def __init__(self, buf, source, sems, places):
        self.buf, self.source, self.sems = buf, source, sems
        self.me, self.core, self.across, self.side, self.mate = places
        self.width = source.shape[0]

    def rows(self, slot, half=None):
        size = self.width if half is None else self.width // 2
        base = slot * self.width + (0 if half is None else half * size)
        return self.buf.at[pl.ds(pl.multiple_of(base, size), size)]

    def copy(self, src, dst, kind, peer):
        return pltpu.make_async_remote_copy(
            src_ref=src,
            dst_ref=dst,
            send_sem=self.sems[0].at[kind, 0],
            recv_sem=self.sems[1].at[kind, 0],
            device_id=peer,
            device_id_type=MESH,
        )

    def to_core(self):
        return self.copy(self.source, self.rows(self.me), 0, {"mp": self.core})

    def to_across(self):
        half = self.width // 2
        cut = self.source.at[pl.ds(pl.multiple_of(self.side * half, half), half)]
        return self.copy(cut, self.rows(self.me, self.side), 1, {"mp": self.across})

    def to_mate(self):
        got = self.rows(self.across, self.side)
        return self.copy(got, got, 2, {"dp": self.mate})

    def onward(self):
        block = self.rows(self.across)
        return self.copy(block, block, 3, {"mp": self.core})

    def start(self):
        self.to_across().start()
        self.to_core().start()

    def relay(self):
        self.to_across().wait_recv()
        self.to_mate().start()

    def forward(self):
        self.to_mate().wait_recv()
        self.onward().start()

    def finish(self):
        self.to_core().wait_recv()
        self.onward().wait_recv()

    def drain(self):
        for c in (self.to_core(), self.to_across(), self.to_mate(), self.onward()):
            c.wait_send()


INPUTS = ("lengths", "res", "cot", "v1", "v2", "v3", "v4", "ib", "be", "w", "wo", "we", "wr")
OUTPUTS = ("out", "grad", "rest", "feed", "small")
IN_VMEM = ("v1", "v2", "v3", "v4", "ib", "be", "small")


class Reduce:
    def __init__(self, buf, first, second, other, sems, dp, size):
        self.buf, self.first, self.second, self.other = buf, first, second, other
        self.sems = sems
        self.high = buf.shape[0] // 2
        self.count = size // 2
        self.piece = self.high // self.count
        self.side = lax.rem(dp, 2)
        self.place = lax.div(dp, 2)
        self.mate = dp + 1 - 2 * self.side

    def rows(self, p, base=0):
        return pl.ds(pl.multiple_of(base + p * self.piece, self.piece), self.piece)

    def own(self, p):
        return self.buf.at[self.rows(p, self.side * self.high)]

    def copy(self, src, dst, stage, p, slot, peer, arrive=None):
        return pltpu.make_async_remote_copy(
            src_ref=src,
            dst_ref=dst,
            send_sem=self.sems[0].at[stage, p],
            recv_sem=self.sems[1].at[stage if arrive is None else arrive, slot],
            device_id={"dp": peer},
            device_id_type=MESH,
        )

    def to_mate(self, p):
        away = self.buf.at[self.rows(p, (1 - self.side) * self.high)]
        return self.copy(away, self.first.at[self.rows(p)], 0, p, p, self.mate)

    def to_owner(self, p, slot):
        return self.copy(
            self.first.at[self.rows(p)], self.second.at[self.rows(slot)], 1, p, slot, 2 * p + self.side
        )

    def onward(self, q, way):
        place = self.place + way
        piece = self.own(q)
        return self.copy(piece, piece, 2 if way > 0 else 4, q, q, 2 * place + self.side, 2)

    def back(self, p):
        return self.copy(self.own(p), self.other.at[self.rows(p)], 3, p, p, self.mate)

    def each(self, body, start=0, stop=None):
        def run(p, _):
            body(p)
            return 0

        lax.fori_loop(start, self.count if stop is None else stop, run, 0)

    def others(self, body):
        def run(p):
            @pl.when(p != self.place)
            def _():
                body(p)

        self.each(run)

    def turn(self, k):
        near = lax.div(k, 2)
        return jnp.where(lax.rem(k, 2) == 0, near, self.count - 1 - near)

    def start(self):
        self.each(lambda k: self.to_mate(self.turn(k)).start())

    def sum_mates(self, p):
        self.to_mate(p).wait_recv()
        here = self.rows(p)
        both = self.buf[self.rows(p, self.side * self.high)].astype(F32) + self.first[here].astype(F32)
        self.first[here] = both.astype(BF16)

        @pl.when(p != self.place)
        def _():
            self.to_owner(p, self.place).start()

    def sum_quarter(self, q):
        self.each(
            lambda k: self.sum_mates(self.turn(k)), q * self.count // 4, (q + 1) * self.count // 4
        )

    def sum_owners(self):
        self.second[self.rows(self.place)] = self.first[self.rows(self.place)]
        self.others(lambda q: self.to_owner(q, q).wait_recv())
        total = lax.fori_loop(
            0,
            self.count,
            lambda q, acc: acc + self.second[self.rows(q)].astype(F32),
            jnp.zeros((self.piece, self.buf.shape[1]), F32),
        )
        self.buf[self.rows(self.place, self.side * self.high)] = total.astype(BF16)
        self.pass_on(self.place, True, True)
        self.back(self.place).start()

    def pass_on(self, q, up, down):
        @pl.when(up & (self.place < self.count - 1))
        def _():
            self.onward(q, 1).start()

        @pl.when(down & (self.place > 0))
        def _():
            self.onward(q, -1).start()

    def forward(self, third):
        def body(d):
            for q, up in ((self.place - d, True), (self.place + d, False)):

                @pl.when((q >= 0) & (q < self.count))
                def _(q=q, up=up):
                    self.onward(q, 1).wait_recv()
                    self.pass_on(q, up, not up)
                    self.back(q).start()

        far = self.count - 1
        self.each(body, 1 + third * far // 3, 1 + (third + 1) * far // 3)

    def finish(self):
        self.each(lambda p: self.back(p).wait_recv())

    def take(self, body):
        for side in range(2):

            @pl.when(self.side == side)
            def _(side=side):
                body(side, self.buf.at[side * self.high : (side + 1) * self.high])
                body(1 - side, self.other)

    def drain(self):
        self.each(lambda p: self.to_mate(p).wait_send())
        self.others(lambda p: self.to_owner(p, self.place).wait_send())
        def sent(q):
            @pl.when((q <= self.place) & (self.place < self.count - 1))
            def _():
                self.onward(q, 1).wait_send()

            @pl.when((q >= self.place) & (self.place > 0))
            def _():
                self.onward(q, -1).wait_send()

        self.each(sent)
        self.each(lambda p: self.back(p).wait_send())


def scratch(count, width, hidden, groups):
    parts = D // width
    blocks = count // SHORT
    bf, f = BF16, F32
    arrays = dict(
        RES=((D, count), bf),
        COT=((D, count), bf),
        MIX=((D, count), bf),
        VIN=((SUBLANES, 2 * LANES), f),
        VEC=((parts, SUBLANES, 2 * LANES), f),
        COLS=((D, LANES), f),
        WO=((D, D), bf),
        WE=((D, hidden), bf),
        WET=((hidden, D), bf),
        WR=((hidden, D), bf),
        WN=((D, 3 * width), bf),
        QT=((width, count), bf),
        KT=((width, count), bf),
        VT=((width, count), bf),
        KN=((count, width), bf),
        VN=((count, width), bf),
        LSE=((blocks, SUBLANES, SHORT), f),
        TOK=((blocks, SUBLANES, SHORT), f),
        X1=((D, count), f),
        E2P=((D, count), bf),
        E2C=((blocks, D // 2, SHORT), bf),
        E2Y=((blocks, D // 2, SHORT), bf),
        E2T=((blocks, D // 2, SHORT), bf),
        PIECES=((2, parts, width, SHORT), bf),
        B2C=((2, blocks, width, SHORT), bf),
        B2Y=((blocks, width, SHORT), bf),
        E1C=((2, blocks, width, SHORT), bf),
        E1Y=((blocks, width, SHORT), bf),
        STAT=((parts, blocks, SUBLANES, SHORT), f),
        GWE=((D, hidden), f),
        GWR=((hidden, D), f),
        GW=((3 * width + width, D), f),
        ACC=((D, LANES), f),
        OWN=((3 * width, LANES), f),
        SQ=((parts, SUBLANES, SHORT), f),
        BM=((2 * D, hidden), bf),
        BM1=((D, hidden), bf),
        BM2=((D, hidden), bf),
        BT=((2 * D, 2 * width), bf),
        SMALL=((groups, 16, 2 * LANES), f),
    )
    sems = dict(
        load=(1, 8), store=(1, 8), bma=(5, groups // 2), bmb=(5, groups // 2), bt=(5, groups // 2), tiny=(1, groups),
        res=(3, blocks), cot=(3, blocks), mix=(3, blocks), wo_=(4, 1), vec_=(3, 1), sq=(3, 1),
        e2a=(1, blocks), e2x=(1, blocks), e2b=(1, blocks),
        b2c=(2, blocks), b2x=(1, blocks), e1c=(2, blocks), e1x=(1, blocks), stat=(3, blocks),
    )
    names, shapes = [], []
    for name, (shape, dtype) in arrays.items():
        names.append(name)
        shapes.append(pltpu.VMEM(shape, dtype))
    for name, shape in sems.items():
        for way in ("s", "r"):
            names.append(f"{name}_{way}")
            shapes.append(pltpu.SemaphoreType.DMA(shape))
    return names, shapes


def layer_kernel(groups, names, *refs):
    n = types.SimpleNamespace(**dict(zip((*INPUTS, *OUTPUTS, *names), refs, strict=True)))
    width, count = n.res.shape
    parts = D // width
    blocks = count // SHORT
    heads = width // HEAD
    hidden = n.we.shape[1]
    me = lax.axis_index("mp")
    core = me + 1 - 2 * lax.rem(me, 2)
    across = lax.rem(me + parts // 2, parts)
    corner = lax.rem(core + parts // 2, parts)
    side = lax.rem(me, 2)
    peers = (core, across, corner)
    dp = lax.axis_index("dp")
    own = at(me, width)

    def tokens(i):
        return at(i, SHORT)

    loads = [
        pltpu.make_async_copy(src, dst, n.load_s.at[0, k])
        for k, (src, dst) in enumerate(
            (
                (n.w, n.BM.at[: 3 * width]),
                (n.wo, n.WO.at[own]),
                (n.res, n.RES.at[own]),
                (n.we, n.WE),
                (n.wr, n.WR),
                (n.cot, n.COT.at[own]),
            )
        )
    ]
    barrier = pltpu.get_barrier_semaphore()
    for peer in peers:
        pl.semaphore_signal(barrier, inc=1, device_id={"mp": peer}, device_id_type=MESH)

    def each_group(body):
        def run(d, _):
            body(d, lax.rem(dp + d, groups))
            return 0

        lax.fori_loop(1, groups, run, 0)

    each_group(
        lambda d, group: pl.semaphore_signal(
            barrier, inc=1, device_id={"dp": group}, device_id_type=MESH
        )
    )
    for c in loads:
        c.start()
    pl.semaphore_wait(barrier, len(peers) + groups - 1)

    feeds = []
    for batch, sems in enumerate(((n.bma_s, n.bma_r), (n.bmb_s, n.bmb_r))):
        cut = slice(batch * 2 * width, (batch + 1) * 2 * width)
        views = [buf.at[:, cut] for buf in (n.BM, n.BM1, n.BM2, n.WET)]
        feeds.append(Reduce(*views, sems, dp, groups))
    feed, feed_late = feeds
    spare = (n.WE.at[:, : 2 * width], n.WE.at[:, 2 * width :], n.WR.at[:, : 2 * width])
    rest = Reduce(n.BT, *spare, (n.bt_s, n.bt_r), dp, groups)

    def gather(buf, source, sems):
        return Gather(
            lambda slot, i: buf.at[at(slot, width), tokens(i)],
            lambda i: source.at[:, tokens(i)],
            sems, me, core, across,
        )

    res = gather(n.RES, n.res, (n.res_s, n.res_r))
    cot = gather(n.COT, n.cot, (n.cot_s, n.cot_r))
    mix = gather(n.MIX, n.MIX.at[own], (n.mix_s, n.mix_r))
    dp_side = lax.rem(dp, 2)
    weight = WeightGather(
        n.WO, n.wo, (n.wo__s, n.wo__r), (me, core, across, dp_side, dp + 1 - 2 * dp_side)
    )

    def vec_copy(k):
        return copy_to(n.VIN, n.VEC.at[me], n.vec__s.at[k, 0], n.vec__r.at[k, 0], peers[k])

    res.start(0)
    n.VIN[...] = jnp.zeros_like(n.VIN)
    for row, source in enumerate((n.v1, n.v2, n.v3, n.v4)):
        n.VIN[row : row + 1, :width] = source[...]
    n.VIN[4:6, :width] = n.ib[...]
    for k in range(3):
        vec_copy(k).start()
    for i in range(1, blocks):
        res.start(i)
    n.VEC[me] = n.VIN[...]
    loads[0].wait()
    n.WN[...] = jnp.transpose(n.BM[: 3 * width])
    for ref in (n.GWE, n.GWR, n.GW, n.ACC, n.OWN, n.SQ):
        ref[...] = jnp.zeros_like(ref)
    total = n.lengths[0, 0]
    for slot in range(1, n.lengths.shape[1]):
        total = total + n.lengths[0, slot]
    far = jnp.where(n.lengths[0, 0] == LONG, 0.0, FAR)
    for c in loads[1:5]:
        c.wait()
    n.WET[...] = jnp.transpose(n.WE[...])
    for k in range(2):
        n.BT[k * D : (k + 1) * D] = jnp.transpose(n.WR[k * 2 * width : (k + 1) * 2 * width])
    for k in range(3):
        vec_copy(k).wait_recv()
    vectors = jnp.concatenate([n.VEC[p][:, :width] for p in range(parts)], axis=1)
    vectors = jnp.where(rows_of(vectors.shape) == 6, n.be[...][None], vectors)
    vectors = jnp.concatenate([vectors, jnp.zeros((LANES - SUBLANES, D), F32)], axis=0)
    n.COLS[...] = jnp.transpose(vectors)
    loads[5].wait()

    def col(k):
        return n.COLS[:, k : k + 1]

    def own_col(k):
        return n.COLS[own, k : k + 1]

    def halves(values):
        pair = values[: 2 * HEAD]
        row = rows_of(pair.shape)
        zero = jnp.zeros_like(pair)
        return (jnp.where(row < HEAD, pair, zero), jnp.where(row < HEAD, zero, pair), values[2 * HEAD :])

    def part_of(values, h):
        return values[:, : 2 * HEAD] if h < 2 else values[:, 2 * HEAD :]

    def head_rows(values, h):
        return values[h * HEAD : (h + 1) * HEAD]

    def forward_block(i, _):
        res.forward(i)

        res.finish(i)
        here = tokens(i)
        full, inverse = decompress(n.RES[:, here].astype(F32))
        rows = (full * inverse * col(0)).astype(BF16)
        qkv = dot(n.BM[: 3 * width], rows)
        q = (qkv[:width] + own_col(4)).astype(BF16)
        k = qkv[width : 2 * width].astype(BF16)
        v = (qkv[2 * width :] + own_col(5)).astype(BF16)
        k_rows = jnp.transpose(k)
        n.QT[:, here] = q
        n.KT[:, here] = k
        n.VT[:, here] = v
        n.KN[here] = k_rows
        n.VN[here] = jnp.transpose(v)
        live = i * SHORT < total
        allowed = diagonal(live)
        q_heads = halves(q * SCORE_SCALE)

        @pl.when(i == blocks - 1)
        def _():
            weight.relay()

        carry = []
        for h in range(heads):
            s = jnp.where(allowed, dot(part_of(k_rows, h), q_heads[h]), -FAR)
            m = jnp.max(s, axis=0, keepdims=True)
            p = jnp.exp(s - m)
            carry.append((m, column_sum(p), dot(head_rows(v, h), p.astype(BF16))))

        def body(j, carry):
            k_j = n.KN[tokens(j)]
            v_j = n.VT[:, tokens(j)]
            after = []
            for h in range(heads):
                m, norm, acc = carry[h]
                s = dot(part_of(k_j, h), q_heads[h])
                new = jnp.maximum(m, jnp.max(s, axis=0, keepdims=True) - far)
                p = jnp.exp(s - (new + far))
                scale = jnp.exp(m - new)
                after.append(
                    (new, norm * scale + column_sum(p), acc * scale + dot(head_rows(v_j, h), p.astype(BF16)))
                )
            return after

        carry = lax.fori_loop(0, i, body, carry)
        mixed = []
        for h in range(heads):
            m, norm, acc = carry[h]
            mixed.append(acc / norm)
            n.LSE[i, h : h + 1] = m + jnp.log(norm)
        n.MIX[own, here] = jnp.concatenate(mixed, axis=0).astype(BF16)


        @pl.when(i == 0)
        def _():
            weight.start()
            mix.start(i)
            cot.start(i)

        return 0

    lax.fori_loop(0, blocks, forward_block, 0)

    high = D // 2

    def e2_half(i, which):
        return n.E2P.at[at(which, high), tokens(i)]

    def e2_first(i):
        return copy_to(e2_half(i, 1 - side), n.E2C.at[i], n.e2a_s.at[0, i], n.e2a_r.at[0, i], core)

    def e2_cross(i):
        return copy_to(n.E2C.at[i], n.E2Y.at[i], n.e2x_s.at[0, i], n.e2x_r.at[0, i], across)

    def e2_last(i):
        return copy_to(e2_half(i, side), n.E2T.at[i], n.e2b_s.at[0, i], n.e2b_r.at[0, i], core)

    def e2_sum(i):
        e2_first(i).wait_recv()
        mine = n.E2P[at(side, high), tokens(i)].astype(F32)
        n.E2C[i] = (mine + n.E2C[i].astype(F32)).astype(BF16)
        e2_cross(i).start()

    def e2_total(i):
        e2_cross(i).wait_recv()
        both = n.E2C[i].astype(F32) + n.E2Y[i].astype(F32)
        n.E2P[at(side, high), tokens(i)] = both.astype(BF16)
        e2_last(i).start()

    def scatter_first(C, sems, slot, i):
        targets = (core, corner)
        return [
            copy_to(
                n.PIECES.at[slot, targets[k]], C.at[k, i], sems[0].at[k, i], sems[1].at[k, i], core
            )
            for k in range(2)
        ]

    def scatter_sum(C, first, slot, i):
        for c in first:
            c.wait_recv()
        for k, owner in enumerate((me, across)):
            C[k, i] = (n.PIECES[slot, owner].astype(F32) + C[k, i].astype(F32)).astype(BF16)

    def scatter_cross(C, Y, sems, i):
        return copy_to(C.at[1, i], Y.at[i], sems[0].at[0, i], sems[1].at[0, i], across)

    def b2_first(slot, i):
        return scatter_first(n.B2C, (n.b2c_s, n.b2c_r), slot, i)

    def b2_cross(i):
        return scatter_cross(n.B2C, n.B2Y, (n.b2x_s, n.b2x_r), i)

    def e1_first(slot, i):
        return scatter_first(n.E1C, (n.e1c_s, n.e1c_r), slot, i)

    def e1_cross(i):
        return scatter_cross(n.E1C, n.E1Y, (n.e1x_s, n.e1x_r), i)

    def split(slot, values):
        for p in range(parts):
            n.PIECES[slot, p] = values[p * width : (p + 1) * width]

    def order(step):
        return lax.rem(blocks - step, blocks)

    for i in range(blocks - 1, 0, -1):
        mix.start(i)
        cot.start(i)
    weight.forward()
    mix.forward(0)
    weight.finish()
    n.BM[D:] = jnp.transpose(n.WO[...])

    def middle_block(step, _):
        i = order(step)
        slot = lax.rem(step, 2)

        @pl.when(step == 1)
        def _():
            mix.forward(i)

        mix.finish(i)
        here = tokens(i)
        full, _unused = decompress(n.RES[:, here].astype(F32))
        x1 = full + center(dot(n.BM[D:], n.MIX[:, here]) + col(1))
        n.X1[:, here] = x1
        rows = (x1 * inverse_rms(x1) * col(2)).astype(BF16)
        z = dot(n.WET[...], rows) + col(6)
        square = z * z
        h = 0.5 + 0.5 * jnp.tanh(z * (0.7978845608 + (0.7978845608 * 0.044715) * square))
        active = z * h
        slope = h + active * (1.0 - h) * (
            2 * 0.7978845608 + (6 * 0.7978845608 * 0.044715) * square
        )
        active = active.astype(BF16)
        slope = slope.astype(BF16)
        cot.forward(i)

        @pl.when(step >= 2)
        def _():
            e2_sum(order(step - 1))
            for c in b2_first(slot, order(step - 2)):
                c.wait_send()

        @pl.when(step >= 1)
        def _():
            before = order(step - 1)
            scatter_sum(n.B2C, b2_first(1 - slot, before), 1 - slot, before)

        b2 = dot(n.BT[:D], active[: 2 * width]) + dot(n.BT[D:], active[2 * width :])
        split(slot, center(b2).astype(BF16))
        for c in b2_first(slot, i):
            c.start()
        cot.finish(i)
        g2 = branch_grad(n.COT[:, here].astype(F32)).astype(BF16)
        n.GWR[...] += dot_nt(active, g2)

        @pl.when((step >= 1) & (step < blocks - 1))
        def _():
            mix.forward(order(step + 1))

        d_hidden = (dot(n.WR[...], g2) * slope).astype(BF16)
        n.ACC[...] += dot(g2, pick(0)) + dot(d_hidden, pick(1))
        n.GWE[...] += dot_nt(rows, d_hidden)
        n.E2P[:, here] = dot(n.WE[...], d_hidden).astype(BF16)
        e2_first(i).start()
        return 0

    lax.fori_loop(0, blocks, middle_block, 0)
    last = (blocks - 1) % 2
    for batch in range(2):
        cut = slice(batch * 2 * width, (batch + 1) * 2 * width)
        n.BM[:D, cut] = n.GWE[:, cut].astype(BF16)
        n.BM[D:, cut] = n.GWR[:, cut].astype(BF16)
        feeds[batch].start()
    e2_sum(order(blocks - 1))
    e2_sum(0)
    scatter_sum(n.B2C, b2_first(last, order(blocks - 1)), last, order(blocks - 1))
    for slot, step in ((1 - last, blocks - 2), (last, blocks - 1)):
        for c in b2_first(slot, order(step)):
            c.wait_send()
    n.GWE[...] = jnp.zeros_like(n.GWE)
    n.GWR[...] = jnp.zeros_like(n.GWR)

    def stat_copy(k, i):
        mine = n.STAT.at[me, i]
        return copy_to(mine, mine, n.stat_s.at[k, i], n.stat_r.at[k, i], peers[k])

    stored = rows_of((width, 1)) + me * width < D - 1

    def finish_grad(i):
        here = tokens(i)
        e1_cross(i).wait_recv()
        for k in range(3):
            stat_copy(k, i).wait_recv()
        stat = n.STAT[0, i]
        for p in range(1, parts):
            stat = stat + n.STAT[p, i]
        along, c_last = stat[0:1], stat[1:2]
        inverse, u_last, g_last = n.TOK[i, 0:1], n.TOK[i, 1:2], n.TOK[i, 2:3]
        e1 = n.E1C[0, i].astype(F32) + n.E1Y[i].astype(F32)
        u_own = jnp.where(stored, n.RES[own, here].astype(F32), u_last)
        normed = e1 * u_own * inverse
        n.OWN[:width] += dot(normed.astype(BF16), pick(3))
        cube = inverse * inverse * inverse * along / D
        result = n.X1[at(across, width), here] + inverse * (e1 * own_col(0)) - u_own * cube
        final = g_last + inverse * c_last - u_last * cube
        n.QT[:, here] = jnp.where(stored, result - final, 0.0).astype(BF16)

    def finish_out(i):
        here = tokens(i)
        b2_cross(i).wait_recv()
        b2 = n.B2C[0, i].astype(F32) + n.B2Y[i].astype(F32)
        x2 = n.X1[own, here] + b2 + (own_col(3) - jnp.mean(col(3), axis=0, keepdims=True))
        n.VT[:, here] = jnp.where(stored, x2, 0.0).astype(BF16)
        live = lanes((1, SHORT)) + i * SHORT < total
        n.SQ[me, 0:1] += jnp.where(live, column_sum(x2 * x2), 0.0)

    def service(point):
        quarters = {1: (feed, 0), 2: (feed, 1), 3: (feed, 2), 4: (feed, 3)}
        quarters |= {5: (feed_late, 0), 6: (feed_late, 1), 8: (feed_late, 2), 9: (feed_late, 3)}
        owners = {9: feed, 14: feed_late}
        thirds = {14: (feed, 0)}
        for table, call in (
            (quarters, lambda entry: entry[0].sum_quarter(entry[1])),
            (owners, lambda entry: entry.sum_owners()),
            (thirds, lambda entry: entry[0].forward(entry[1])),
        ):
            for when, entry in table.items():

                @pl.when(point == when)
                def _(call=call, entry=entry):
                    call(entry)

    def backward_block(step, _):
        i = blocks - 1 - step
        slot = lax.rem(step, 2)
        here = tokens(i)

        @pl.when(step == 0)
        def _():
            e2_total(i)

        @pl.when(step == 1)
        def _():
            for b in range(blocks):
                b2_cross(b).start()

        e2_last(i).wait_recv()
        e2_first(i).wait_send()
        n.E2P[at(1 - side, high), here] = n.E2T[i]
        x1 = n.X1[:, here]
        inverse = inverse_rms(x1)
        e2 = n.E2P[:, here].astype(F32)
        normed = e2 * x1
        gain_part = (normed * inverse).astype(BF16)
        along = column_sum(normed * col(2))
        du = inverse * (e2 * col(2)) - x1 * (inverse * inverse * inverse * along / D)
        g1 = branch_grad(n.COT[:, here].astype(F32)) + center(du)
        n.TOK[i, 2:3] = g1[D - 1 :]
        for p in range(parts):

            @pl.when(me == p)
            def _():
                n.X1[at(across, width), here] = g1[p * width : (p + 1) * width]

        g1 = g1.astype(BF16)
        n.ACC[...] += dot(gain_part, pick(2)) + dot(g1, pick(3))
        mixed = n.MIX[own, here]
        n.GW[3 * width :] += dot_nt(mixed, g1)
        d_mixed = dot(n.WO[own], g1).astype(BF16)
        service(5 * step)
        product = d_mixed.astype(F32) * mixed.astype(F32)
        delta = [column_sum(head_rows(product, h)) for h in range(heads)]
        lse = [n.LSE[i, h : h + 1] for h in range(heads)]
        live = i * SHORT < total
        q = n.QT[:, here] * SCORE_SCALE
        q_heads = halves(q)
        g_heads = halves(d_mixed)

        def pair(j, lse, allowed):
            there = tokens(j)
            k_j, v_j, k_t = n.KN[there], n.VN[there], n.KT[:, there]
            dq, dk, dv = [], [], []
            for h in range(heads):
                p = jnp.exp(dot(part_of(k_j, h), q_heads[h]) - lse[h])
                if allowed is not None:
                    p = jnp.where(allowed, p, 0.0)
                dv.append(dot_nt(head_rows(d_mixed, h), p.astype(BF16)))
                p = (p * (dot(part_of(v_j, h), g_heads[h]) - delta[h])).astype(BF16)
                dk.append(dot_nt(head_rows(q, h), p))
                dq.append(dot(head_rows(k_t, h), p))
            n.GWE[at(j, width), :SHORT] += jnp.concatenate(dv, axis=0)
            n.GWR[at(j, width), :SHORT] += jnp.concatenate(dk, axis=0)
            return jnp.concatenate(dq, axis=0)

        dq = pair(i, lse, diagonal(live))

        @pl.when(i >= 1)
        def _():
            e2_total(i - 1)

        service(5 * step + 1)

        @pl.when(step >= 1)
        def _():
            scatter_sum(n.E1C, e1_first(1 - slot, i + 1), 1 - slot, i + 1)
            e1_cross(i + 1).start()

        lse_far = [row + far for row in lse]

        def body(j, dq):
            dq = dq + pair(j, lse_far, None)

            @pl.when(j <= 1)
            def _():
                service(5 * step + 2 + j)

            return dq

        dq = lax.fori_loop(0, i, body, dq)
        d_all = jnp.concatenate(
            [dq * SCORE_SCALE, n.GWR[at(i, width), :SHORT], n.GWE[at(i, width), :SHORT]], axis=0
        ).astype(BF16)
        n.OWN[...] += dot(d_all, pick(0))
        full, inverse = decompress(n.RES[:, here].astype(F32))
        rows = (full * inverse * col(0)).astype(BF16)
        n.GW[: 3 * width] += dot_nt(d_all, rows)
        e1 = dot(n.WN[...], d_all)

        @pl.when(step >= 2)
        def _():
            for c in e1_first(slot, i + 2):
                c.wait_send()

        split(slot, e1.astype(BF16))
        for c in e1_first(slot, i):
            c.start()
        c = e1 * col(0)
        n.STAT[me, i, 0:1] = column_sum(c * full)
        n.STAT[me, i, 1:2] = c[D - 1 :]
        for k in range(3):
            stat_copy(k, i).start()
        n.TOK[i, 0:1] = inverse
        n.TOK[i, 1:2] = full[D - 1 :]
        service(5 * step + 4)
        return 0

    lax.fori_loop(0, blocks, backward_block, 0)
    scatter_sum(n.E1C, e1_first(last, 0), last, 0)
    e1_cross(0).start()
    n.BT[:D] = n.GW[:, : 2 * width].astype(BF16)
    n.BT[D:] = n.GW[:, 2 * width :].astype(BF16)
    rest.start()
    feed.forward(1)
    feed.forward(2)
    for third in range(3):
        feed_late.forward(third)

    def square_copy(k):
        return copy_to(n.SQ.at[me], n.SQ.at[me], n.sq_s.at[k, 0], n.sq_r.at[k, 0], peers[k])

    def finish_block(k, _):
        finish_out(k)
        rest.sum_quarter(k)
        return 0

    lax.fori_loop(0, blocks, finish_block, 0)
    for k in range(3):
        square_copy(k).start()

    def finish_rows(k, _):
        finish_grad(blocks - 1 - k)
        return 0

    rest.sum_owners()
    lax.fori_loop(0, blocks, finish_rows, 0)
    for k in range(3):
        square_copy(k).wait_recv()

    def tiny_copy(slot, group):
        here = n.SMALL.at[dp]
        return pltpu.make_async_remote_copy(
            src_ref=here,
            dst_ref=here,
            send_sem=n.tiny_s.at[0, group],
            recv_sem=n.tiny_r.at[0, slot],
            device_id={"dp": group},
            device_id_type=MESH,
        )

    squares = jnp.sum(sum(n.SQ[p, 0:1] for p in range(parts)), axis=1, keepdims=True)
    mine = n.ACC[own]
    parts_in = [
        n.OWN[:width, 0:1],
        n.OWN[2 * width :, 0:1],
        n.OWN[:width, 3:4],
        squares,
        mine[:, 3:4],
        mine[:, 2:3],
        mine[:, 0:1],
        total.astype(F32),
    ] + [n.ACC[p * width : (p + 1) * width, 1:2] for p in range(parts)]
    table = jnp.zeros((width, LANES), F32)
    for lane, values in enumerate(parts_in):
        table = jnp.where(lanes(table.shape) == lane, values, table)
    table = jnp.concatenate([table, jnp.zeros((2 * LANES - width, LANES), F32)], axis=0)
    n.SMALL[dp] = jnp.transpose(table)[:16]
    each_group(lambda d, group: tiny_copy(dp, group).start())

    def store(src, dst, k):
        return pltpu.make_async_copy(src, dst, n.store_s.at[0, k])

    stores = [store(n.QT, n.grad, 0), store(n.VT, n.out, 1)]
    for c in stores:
        c.start()
    each_group(lambda d, group: tiny_copy(group, group).wait_recv())
    small = n.SMALL[0]
    for group in range(1, groups):
        small = small + n.SMALL[group]
    n.small[...] = small

    def store_batch(batch, target, k):
        batch.finish()

        def body(half, rows):
            store(rows, target.at[half * D : (half + 1) * D], k + half).start()

        batch.take(body)
        for half in range(2):
            here = slice(half * D, (half + 1) * D)
            stores.append(store(batch.buf.at[here], target.at[here], k + half))

    rest.forward(0)
    store_batch(feed, n.feed.at[:, : 2 * width], 2)
    rest.forward(1)
    store_batch(feed_late, n.feed.at[:, 2 * width :], 4)
    rest.forward(2)
    store_batch(rest, n.rest, 6)

    for k in range(3):
        vec_copy(k).wait_send()
        square_copy(k).wait_send()
    weight.drain()

    def drain(i, _):
        for g in (res, cot, mix):
            g.drain(i)
        for c in (e2_cross, e2_last, b2_cross, e1_cross):
            c(i).wait_send()
        for k in range(3):
            stat_copy(k, i).wait_send()
        return 0

    lax.fori_loop(0, blocks, drain, 0)
    for step in (blocks - 2, blocks - 1):
        for c in e1_first(step % 2, blocks - 1 - step):
            c.wait_send()
    for c in stores:
        c.wait()
    for batch in (feed, feed_late, rest):
        batch.drain()
    each_group(lambda d, group: tiny_copy(dp, group).wait_send())


def finish_kernel(
    out, grad, rest_low, rest_high, feed_low, feed_high, small,
    out_ref, grad_ref, gw_ref, gwo_ref, gwe_ref, gwr_ref,
    gb_ref, gbo_ref, gg_one_ref, gg_two_ref, gbe_ref, gbr_ref, rms_ref, live_ref,
):
    i = pl.program_id(0)
    width = gb_ref.shape[1]
    out_ref[...] = out[...]
    grad_ref[...] = grad[...]
    rest = jnp.concatenate([rest_low[...], rest_high[...]], axis=1).astype(F32)
    gwe_ref[...] = feed_low[...].astype(F32)
    gwr_ref[...] = feed_high[...].astype(F32)

    most = pl.num_programs(0) * 3 // 4

    @pl.when(i < most)
    def _():
        gw_ref[...] = rest

    @pl.when(i >= most)
    def _():
        gwo_ref[...] = rest

    @pl.when(i == 0)
    def _():
        gb_ref[...] = small[0:2, :width]
        gg_one_ref[...] = small[2, :width]
        gbo_ref[...] = small[4, :width]
        gg_two_ref[...] = small[5, :width]
        gbr_ref[...] = small[6, :width]
        for p in range(D // width):
            gbe_ref[p * width : (p + 1) * width] = small[8 + p, :width]
        live = small[7:8, 0:1]
        rms_ref[...] = jnp.sqrt(small[3:4, 0:1] / (D * live))
        live_ref[...] = live.astype(jnp.int32)


def on_device(
    residual,
    lengths,
    gain_one,
    input_weight,
    input_bias,
    output_weight,
    output_bias,
    gain_two,
    expand_weight,
    expand_bias,
    reduce_weight,
    reduce_bias,
    cotangent,
):
    count, width = residual.shape
    hidden = expand_weight.shape[1]
    parts = D // width

    def shape(*dims, dtype=F32):
        return jax.ShapeDtypeStruct(dims, dtype)

    groups = lax.axis_size("dp")
    names, scratches = scratch(count, width, hidden, groups)

    def space(name):
        return pl.BlockSpec(memory_space=pltpu.VMEM if name in IN_VMEM else pl.ANY)

    out, grad, rest, feed, small = pl.pallas_call(
        lambda *refs: layer_kernel(groups, names, *refs),
        in_specs=[pl.BlockSpec(memory_space=pltpu.SMEM)] + [space(name) for name in INPUTS[1:]],
        out_specs=[space(name) for name in OUTPUTS],
        out_shape=[
            shape(width, count, dtype=BF16),
            shape(width, count, dtype=BF16),
            shape(2 * D, 2 * width, dtype=BF16),
            shape(2 * D, hidden, dtype=BF16),
            shape(16, 2 * LANES),
        ],
        scratch_shapes=scratches,
        compiler_params=pltpu.CompilerParams(
            vmem_limit_bytes=63 << 20, collective_id=0, has_side_effects=True
        ),
        name="layer",
    )(
        lengths,
        residual.T,
        cotangent.T,
        gain_one[None],
        output_bias[None],
        gain_two[None],
        reduce_bias[None],
        input_bias,
        expand_bias,
        jnp.transpose(input_weight, (0, 2, 1)).reshape(3 * width, D),
        output_weight,
        expand_weight,
        reduce_weight,
    )

    def rows(high, wide, base=0):
        return pl.BlockSpec((high, wide), lambda i: (i + base, 0))

    def whole(*dims):
        return pl.BlockSpec(dims, lambda i: (0,) * len(dims))

    def clip(high, wide, first, last):
        return pl.BlockSpec((high, wide), lambda i: (jnp.clip(i - first, 0, last - first), 0))

    steps = parts
    step = D // steps
    thin = width // steps
    out, grad, gw, gwo, gwe, gwr, *vectors = pl.pallas_call(
        finish_kernel,
        grid=(steps,),
        in_specs=[
            rows(thin, count),
            rows(thin, count),
            rows(step, 2 * width),
            rows(step, 2 * width, steps),
            rows(step, hidden),
            rows(step, hidden, steps),
            whole(16, 2 * LANES),
        ],
        out_specs=[
            rows(thin, count),
            rows(thin, count),
            clip(step, D, 0, steps * 3 // 4 - 1),
            clip(step, D, steps * 3 // 4, steps - 1),
            rows(step, hidden),
            rows(step, hidden),
            whole(2, width),
            whole(width),
            whole(width),
            whole(width),
            whole(hidden),
            whole(width),
            whole(1, 1),
            whole(1, 1),
        ],
        out_shape=[
            shape(width, count, dtype=BF16),
            shape(width, count, dtype=BF16),
            shape(3 * width, D),
            shape(width, D),
            shape(D, hidden),
            shape(hidden, D),
            shape(2, width),
            shape(width),
            shape(width),
            shape(width),
            shape(hidden),
            shape(width),
            shape(1, 1),
            shape(1, 1, dtype=jnp.int32),
        ],
        compiler_params=pltpu.CompilerParams(vmem_limit_bytes=60 << 20),
        name="finish",
    )(out, grad, rest, rest, feed, feed, small)
    gb, gbo, gg_one, gg_two, gbe, gbr, rms, live_count = vectors
    return (
        out.T,
        grad.T,
        jnp.transpose(gw.reshape(3, width, D), (0, 2, 1)),
        gb,
        gwo,
        gbo,
        gg_one,
        gg_two,
        gwe,
        gbe,
        gwr,
        gbr,
        rms[0, 0],
        live_count[0, 0],
    )


def solution(mesh):
    return jax.shard_map(
        on_device,
        mesh=mesh,
        in_specs=(
            P("dp", "mp"),
            P("dp", None),
            P("mp"),
            P(None, None, "mp"),
            P(None, "mp"),
            P("mp", None),
            P("mp"),
            P("mp"),
            P(None, "mp"),
            P("mp"),
            P("mp", None),
            P("mp"),
            P("dp", "mp"),
        ),
        out_specs=(
            P("dp", "mp"),
            P("dp", "mp"),
            P(None, None, "mp"),
            P(None, "mp"),
            P("mp", None),
            P("mp"),
            P("mp"),
            P("mp"),
            P(None, "mp"),
            P("mp"),
            P("mp", None),
            P("mp"),
            P(),
            P(),
        ),
        check_vma=False,
    )
```

```python
import types

import jax
import jax.numpy as jnp
from jax import lax
from jax.experimental import pallas as pl
from jax.experimental.pallas import tpu as pltpu
from jax.sharding import PartitionSpec as P


D = 768
HEAD = 64
SHORT = 512
LONG = 2048
EPSILON = 1e-05
SCORE_SCALE = 0.125
FAR = 1e30
LANES = 128
SUBLANES = 8
MESH = pl.DeviceIdType.MESH

F32 = jnp.float32
BF16 = jnp.bfloat16
NT = (((1,), (1,)), ((), ()))


def dot(a, b):
    return jnp.dot(a, b, preferred_element_type=F32)


def dot_nt(a, b):
    return lax.dot_general(a, b, NT, preferred_element_type=F32)


def lanes(shape):
    return lax.broadcasted_iota(jnp.int32, shape, 1)


def rows_of(shape):
    return lax.broadcasted_iota(jnp.int32, shape, 0)


def at(index, size):
    return pl.ds(pl.multiple_of(index * size, size), size)


def column_sum(values):
    return jnp.sum(values, axis=0, keepdims=True)


def with_last(values, last):
    cut = values.shape[0] - SUBLANES
    end = values[cut:]
    end = jnp.where(rows_of(end.shape) == SUBLANES - 1, last, end)
    return jnp.concatenate([values[:cut], end], axis=0)


def decompress(raw):
    full = with_last(raw, 0.0)
    full = with_last(full, -column_sum(full))
    return full, inverse_rms(full)


def inverse_rms(full):
    return lax.rsqrt(column_sum(full * full) / D + EPSILON)


def center(values):
    return values - column_sum(values) / D


def branch_grad(raw):
    return center(with_last(raw, 0.0))


def diagonal(live):
    key = rows_of((SHORT, SHORT))
    query = lanes((SHORT, SHORT))
    return (key == query) | ((key < query) & live)


def pick(lane):
    return (lanes((SHORT, LANES)) == lane).astype(BF16)


def copy_to(src, dst, send_sem, recv_sem, peer):
    return pltpu.make_async_remote_copy(
        src_ref=src,
        dst_ref=dst,
        send_sem=send_sem,
        recv_sem=recv_sem,
        device_id={"mp": peer},
        device_id_type=MESH,
    )


class Gather:
    def __init__(self, piece, source, sems, me, core, across):
        self.piece, self.source = piece, source
        self.me, self.core, self.across = me, core, across
        self.send, self.recv = sems

    def copy(self, kind, i):
        slot = self.across if kind == 2 else self.me
        peer = self.across if kind == 1 else self.core
        there = self.piece(slot, i)
        here = there if kind == 2 else self.source(i)
        return copy_to(here, there, self.send.at[kind, i], self.recv.at[kind, i], peer)

    def start(self, i):
        self.copy(1, i).start()
        self.copy(0, i).start()

    def forward(self, i):
        self.copy(1, i).wait_recv()
        self.copy(2, i).start()

    def finish(self, i):
        self.copy(0, i).wait_recv()
        self.copy(2, i).wait_recv()

    def drain(self, i):
        for kind in range(3):
            self.copy(kind, i).wait_send()


class WeightGather:
    def __init__(self, buf, source, sems, places):
        self.buf, self.source, self.sems = buf, source, sems
        self.me, self.core, self.across, self.side, self.mate = places
        self.width = source.shape[0]

    def rows(self, slot, half=None):
        size = self.width if half is None else self.width // 2
        base = slot * self.width + (0 if half is None else half * size)
        return self.buf.at[pl.ds(pl.multiple_of(base, size), size)]

    def copy(self, src, dst, kind, peer):
        return pltpu.make_async_remote_copy(
            src_ref=src,
            dst_ref=dst,
            send_sem=self.sems[0].at[kind, 0],
            recv_sem=self.sems[1].at[kind, 0],
            device_id=peer,
            device_id_type=MESH,
        )

    def to_core(self):
        return self.copy(self.source, self.rows(self.me), 0, {"mp": self.core})

    def to_across(self):
        half = self.width // 2
        cut = self.source.at[pl.ds(pl.multiple_of(self.side * half, half), half)]
        return self.copy(cut, self.rows(self.me, self.side), 1, {"mp": self.across})

    def to_mate(self):
        got = self.rows(self.across, self.side)
        return self.copy(got, got, 2, {"dp": self.mate})

    def onward(self):
        block = self.rows(self.across)
        return self.copy(block, block, 3, {"mp": self.core})

    def start(self):
        self.to_across().start()
        self.to_core().start()

    def relay(self):
        self.to_across().wait_recv()
        self.to_mate().start()

    def forward(self):
        self.to_mate().wait_recv()
        self.onward().start()

    def finish(self):
        self.to_core().wait_recv()
        self.onward().wait_recv()

    def drain(self):
        for c in (self.to_core(), self.to_across(), self.to_mate(), self.onward()):
            c.wait_send()


INPUTS = ("lengths", "res", "cot", "v1", "v2", "v3", "v4", "ib", "be", "w", "wo", "we", "wr")
OUTPUTS = ("out", "grad", "rest", "feed", "small")
IN_VMEM = ("v1", "v2", "v3", "v4", "ib", "be", "small")


class Reduce:
    def __init__(self, buf, first, second, other, sems, dp, size):
        self.buf, self.first, self.second, self.other = buf, first, second, other
        self.sems = sems
        self.high = buf.shape[0] // 2
        self.count = size // 2
        self.piece = self.high // self.count
        self.side = lax.rem(dp, 2)
        self.place = lax.div(dp, 2)
        self.mate = dp + 1 - 2 * self.side

    def rows(self, p, base=0):
        return pl.ds(pl.multiple_of(base + p * self.piece, self.piece), self.piece)

    def own(self, p):
        return self.buf.at[self.rows(p, self.side * self.high)]

    def copy(self, src, dst, stage, p, slot, peer, arrive=None):
        return pltpu.make_async_remote_copy(
            src_ref=src,
            dst_ref=dst,
            send_sem=self.sems[0].at[stage, p],
            recv_sem=self.sems[1].at[stage if arrive is None else arrive, slot],
            device_id={"dp": peer},
            device_id_type=MESH,
        )

    def to_mate(self, p):
        away = self.buf.at[self.rows(p, (1 - self.side) * self.high)]
        return self.copy(away, self.first.at[self.rows(p)], 0, p, p, self.mate)

    def to_owner(self, p, slot):
        return self.copy(
            self.first.at[self.rows(p)], self.second.at[self.rows(slot)], 1, p, slot, 2 * p + self.side
        )

    def onward(self, q, way):
        place = self.place + way
        piece = self.own(q)
        return self.copy(piece, piece, 2 if way > 0 else 4, q, q, 2 * place + self.side, 2)

    def back(self, p):
        return self.copy(self.own(p), self.other.at[self.rows(p)], 3, p, p, self.mate)

    def each(self, body, start=0, stop=None):
        def run(p, _):
            body(p)
            return 0

        lax.fori_loop(start, self.count if stop is None else stop, run, 0)

    def others(self, body):
        def run(p):
            @pl.when(p != self.place)
            def _():
                body(p)

        self.each(run)

    def turn(self, k):
        near = lax.div(k, 2)
        return jnp.where(lax.rem(k, 2) == 0, near, self.count - 1 - near)

    def start(self):
        self.each(lambda k: self.to_mate(self.turn(k)).start())

    def sum_mates(self, p):
        self.to_mate(p).wait_recv()
        here = self.rows(p)
        both = self.buf[self.rows(p, self.side * self.high)].astype(F32) + self.first[here].astype(F32)
        self.first[here] = both.astype(BF16)

        @pl.when(p != self.place)
        def _():
            self.to_owner(p, self.place).start()

    def sum_quarter(self, q):
        self.each(
            lambda k: self.sum_mates(self.turn(k)), q * self.count // 4, (q + 1) * self.count // 4
        )

    def sum_owners(self):
        self.second[self.rows(self.place)] = self.first[self.rows(self.place)]
        self.others(lambda q: self.to_owner(q, q).wait_recv())
        total = lax.fori_loop(
            0,
            self.count,
            lambda q, acc: acc + self.second[self.rows(q)].astype(F32),
            jnp.zeros((self.piece, self.buf.shape[1]), F32),
        )
        self.buf[self.rows(self.place, self.side * self.high)] = total.astype(BF16)
        self.pass_on(self.place, True, True)
        self.back(self.place).start()

    def pass_on(self, q, up, down):
        @pl.when(up & (self.place < self.count - 1))
        def _():
            self.onward(q, 1).start()

        @pl.when(down & (self.place > 0))
        def _():
            self.onward(q, -1).start()

    def forward(self, third):
        def body(d):
            for q, up in ((self.place - d, True), (self.place + d, False)):

                @pl.when((q >= 0) & (q < self.count))
                def _(q=q, up=up):
                    self.onward(q, 1).wait_recv()
                    self.pass_on(q, up, not up)
                    self.back(q).start()

        far = self.count - 1
        self.each(body, 1 + third * far // 3, 1 + (third + 1) * far // 3)

    def finish(self):
        self.each(lambda p: self.back(p).wait_recv())

    def take(self, body):
        for side in range(2):

            @pl.when(self.side == side)
            def _(side=side):
                body(side, self.buf.at[side * self.high : (side + 1) * self.high])
                body(1 - side, self.other)

    def drain(self):
        self.each(lambda p: self.to_mate(p).wait_send())
        self.others(lambda p: self.to_owner(p, self.place).wait_send())
        def sent(q):
            @pl.when((q <= self.place) & (self.place < self.count - 1))
            def _():
                self.onward(q, 1).wait_send()

            @pl.when((q >= self.place) & (self.place > 0))
            def _():
                self.onward(q, -1).wait_send()

        self.each(sent)
        self.each(lambda p: self.back(p).wait_send())


def scratch(count, width, hidden, groups):
    parts = D // width
    blocks = count // SHORT
    bf, f = BF16, F32
    arrays = dict(
        RES=((D, count), bf),
        COT=((D, count), bf),
        MIX=((D, count), bf),
        VIN=((SUBLANES, 2 * LANES), f),
        VEC=((parts, SUBLANES, 2 * LANES), f),
        COLS=((D, LANES), f),
        WO=((D, D), bf),
        WE=((D, hidden), bf),
        WET=((hidden, D), bf),
        WR=((hidden, D), bf),
        WN=((D, 3 * width), bf),
        QT=((width, count), bf),
        KT=((width, count), bf),
        VT=((width, count), bf),
        KN=((count, width), bf),
        VN=((count, width), bf),
        LSE=((blocks, SUBLANES, SHORT), f),
        TOK=((blocks, SUBLANES, SHORT), f),
        X1=((D, count), f),
        E2P=((D, count), bf),
        E2C=((blocks, D // 2, SHORT), bf),
        E2Y=((blocks, D // 2, SHORT), bf),
        E2T=((blocks, D // 2, SHORT), bf),
        PIECES=((2, parts, width, SHORT), bf),
        B2C=((2, blocks, width, SHORT), bf),
        B2Y=((blocks, width, SHORT), bf),
        E1C=((2, blocks, width, SHORT), bf),
        E1Y=((blocks, width, SHORT), bf),
        STAT=((parts, blocks, SUBLANES, SHORT), f),
        GWE=((D, hidden), f),
        GWR=((hidden, D), f),
        GW=((3 * width + width, D), f),
        ACC=((D, LANES), f),
        OWN=((3 * width, LANES), f),
        SQ=((parts, SUBLANES, SHORT), f),
        BM=((2 * D, hidden), bf),
        BM1=((D, hidden), bf),
        BM2=((D, hidden), bf),
        BT=((2 * D, 2 * width), bf),
        SMALL=((groups, 16, 2 * LANES), f),
    )
    sems = dict(
        load=(1, 8), store=(1, 8), bma=(5, groups // 2), bmb=(5, groups // 2), bt=(5, groups // 2), tiny=(1, groups),
        res=(3, blocks), cot=(3, blocks), mix=(3, blocks), wo_=(4, 1), vec_=(3, 1), sq=(3, 1),
        e2a=(1, blocks), e2x=(1, blocks), e2b=(1, blocks),
        b2c=(2, blocks), b2x=(1, blocks), e1c=(2, blocks), e1x=(1, blocks), stat=(3, blocks),
    )
    names, shapes = [], []
    for name, (shape, dtype) in arrays.items():
        names.append(name)
        shapes.append(pltpu.VMEM(shape, dtype))
    for name, shape in sems.items():
        for way in ("s", "r"):
            names.append(f"{name}_{way}")
            shapes.append(pltpu.SemaphoreType.DMA(shape))
    return names, shapes


def layer_kernel(groups, names, *refs):
    n = types.SimpleNamespace(**dict(zip((*INPUTS, *OUTPUTS, *names), refs, strict=True)))
    width, count = n.res.shape
    parts = D // width
    blocks = count // SHORT
    heads = width // HEAD
    hidden = n.we.shape[1]
    me = lax.axis_index("mp")
    core = me + 1 - 2 * lax.rem(me, 2)
    across = lax.rem(me + parts // 2, parts)
    corner = lax.rem(core + parts // 2, parts)
    side = lax.rem(me, 2)
    peers = (core, across, corner)
    dp = lax.axis_index("dp")
    own = at(me, width)

    def tokens(i):
        return at(i, SHORT)

    loads = [
        pltpu.make_async_copy(src, dst, n.load_s.at[0, k])
        for k, (src, dst) in enumerate(
            (
                (n.w, n.BM.at[: 3 * width]),
                (n.wo, n.WO.at[own]),
                (n.res, n.RES.at[own]),
                (n.we, n.WE),
                (n.wr, n.WR),
                (n.cot, n.COT.at[own]),
            )
        )
    ]
    barrier = pltpu.get_barrier_semaphore()
    for peer in peers:
        pl.semaphore_signal(barrier, inc=1, device_id={"mp": peer}, device_id_type=MESH)

    def each_group(body):
        def run(d, _):
            body(d, lax.rem(dp + d, groups))
            return 0

        lax.fori_loop(1, groups, run, 0)

    each_group(
        lambda d, group: pl.semaphore_signal(
            barrier, inc=1, device_id={"dp": group}, device_id_type=MESH
        )
    )
    for c in loads:
        c.start()
    pl.semaphore_wait(barrier, len(peers) + groups - 1)

    feeds = []
    for batch, sems in enumerate(((n.bma_s, n.bma_r), (n.bmb_s, n.bmb_r))):
        cut = slice(batch * 2 * width, (batch + 1) * 2 * width)
        views = [buf.at[:, cut] for buf in (n.BM, n.BM1, n.BM2, n.WET)]
        feeds.append(Reduce(*views, sems, dp, groups))
    feed, feed_late = feeds
    spare = (n.WE.at[:, : 2 * width], n.WE.at[:, 2 * width :], n.WR.at[:, : 2 * width])
    rest = Reduce(n.BT, *spare, (n.bt_s, n.bt_r), dp, groups)

    def gather(buf, source, sems):
        return Gather(
            lambda slot, i: buf.at[at(slot, width), tokens(i)],
            lambda i: source.at[:, tokens(i)],
            sems, me, core, across,
        )

    res = gather(n.RES, n.res, (n.res_s, n.res_r))
    cot = gather(n.COT, n.cot, (n.cot_s, n.cot_r))
    mix = gather(n.MIX, n.MIX.at[own], (n.mix_s, n.mix_r))
    dp_side = lax.rem(dp, 2)
    weight = WeightGather(
        n.WO, n.wo, (n.wo__s, n.wo__r), (me, core, across, dp_side, dp + 1 - 2 * dp_side)
    )

    def vec_copy(k):
        return copy_to(n.VIN, n.VEC.at[me], n.vec__s.at[k, 0], n.vec__r.at[k, 0], peers[k])

    res.start(0)
    n.VIN[...] = jnp.zeros_like(n.VIN)
    for row, source in enumerate((n.v1, n.v2, n.v3, n.v4)):
        n.VIN[row : row + 1, :width] = source[...]
    n.VIN[4:6, :width] = n.ib[...]
    for k in range(3):
        vec_copy(k).start()
    for i in range(1, blocks):
        res.start(i)
    n.VEC[me] = n.VIN[...]
    loads[0].wait()
    n.WN[...] = jnp.transpose(n.BM[: 3 * width])
    for ref in (n.GWE, n.GWR, n.GW, n.ACC, n.OWN, n.SQ):
        ref[...] = jnp.zeros_like(ref)
    total = n.lengths[0, 0]
    for slot in range(1, n.lengths.shape[1]):
        total = total + n.lengths[0, slot]
    far = jnp.where(n.lengths[0, 0] == LONG, 0.0, FAR)
    for c in loads[1:5]:
        c.wait()
    n.WET[...] = jnp.transpose(n.WE[...])
    for k in range(2):
        n.BT[k * D : (k + 1) * D] = jnp.transpose(n.WR[k * 2 * width : (k + 1) * 2 * width])
    for k in range(3):
        vec_copy(k).wait_recv()
    vectors = jnp.concatenate([n.VEC[p][:, :width] for p in range(parts)], axis=1)
    vectors = jnp.where(rows_of(vectors.shape) == 6, n.be[...][None], vectors)
    vectors = jnp.concatenate([vectors, jnp.zeros((LANES - SUBLANES, D), F32)], axis=0)
    n.COLS[...] = jnp.transpose(vectors)
    loads[5].wait()

    def col(k):
        return n.COLS[:, k : k + 1]

    def own_col(k):
        return n.COLS[own, k : k + 1]

    def halves(values):
        pair = values[: 2 * HEAD]
        row = rows_of(pair.shape)
        zero = jnp.zeros_like(pair)
        return (jnp.where(row < HEAD, pair, zero), jnp.where(row < HEAD, zero, pair), values[2 * HEAD :])

    def part_of(values, h):
        return values[:, : 2 * HEAD] if h < 2 else values[:, 2 * HEAD :]

    def head_rows(values, h):
        return values[h * HEAD : (h + 1) * HEAD]

    def forward_block(i, _):
        res.forward(i)

        res.finish(i)
        here = tokens(i)
        full, inverse = decompress(n.RES[:, here].astype(F32))
        rows = (full * inverse * col(0)).astype(BF16)
        qkv = dot(n.BM[: 3 * width], rows)
        q = (qkv[:width] + own_col(4)).astype(BF16)
        k = qkv[width : 2 * width].astype(BF16)
        v = (qkv[2 * width :] + own_col(5)).astype(BF16)
        k_rows = jnp.transpose(k)
        n.QT[:, here] = q
        n.KT[:, here] = k
        n.VT[:, here] = v
        n.KN[here] = k_rows
        n.VN[here] = jnp.transpose(v)
        live = i * SHORT < total
        allowed = diagonal(live)
        q_heads = halves(q * SCORE_SCALE)

        @pl.when(i == blocks - 1)
        def _():
            weight.relay()

        carry = []
        for h in range(heads):
            s = jnp.where(allowed, dot(part_of(k_rows, h), q_heads[h]), -FAR)
            m = jnp.max(s, axis=0, keepdims=True)
            p = jnp.exp(s - m)
            carry.append((m, column_sum(p), dot(head_rows(v, h), p.astype(BF16))))

        def body(j, carry):
            k_j = n.KN[tokens(j)]
            v_j = n.VT[:, tokens(j)]
            after = []
            for h in range(heads):
                m, norm, acc = carry[h]
                s = dot(part_of(k_j, h), q_heads[h])
                new = jnp.maximum(m, jnp.max(s, axis=0, keepdims=True) - far)
                p = jnp.exp(s - (new + far))
                scale = jnp.exp(m - new)
                after.append(
                    (new, norm * scale + column_sum(p), acc * scale + dot(head_rows(v_j, h), p.astype(BF16)))
                )
            return after

        carry = lax.fori_loop(0, i, body, carry)
        mixed = []
        for h in range(heads):
            m, norm, acc = carry[h]
            mixed.append(acc / norm)
            n.LSE[i, h : h + 1] = m + jnp.log(norm)
        n.MIX[own, here] = jnp.concatenate(mixed, axis=0).astype(BF16)


        @pl.when(i == 0)
        def _():
            weight.start()
            mix.start(i)
            cot.start(i)

        return 0

    lax.fori_loop(0, blocks, forward_block, 0)

    high = D // 2

    def e2_half(i, which):
        return n.E2P.at[at(which, high), tokens(i)]

    def e2_first(i):
        return copy_to(e2_half(i, 1 - side), n.E2C.at[i], n.e2a_s.at[0, i], n.e2a_r.at[0, i], core)

    def e2_cross(i):
        return copy_to(n.E2C.at[i], n.E2Y.at[i], n.e2x_s.at[0, i], n.e2x_r.at[0, i], across)

    def e2_last(i):
        return copy_to(e2_half(i, side), n.E2T.at[i], n.e2b_s.at[0, i], n.e2b_r.at[0, i], core)

    def e2_sum(i):
        e2_first(i).wait_recv()
        mine = n.E2P[at(side, high), tokens(i)].astype(F32)
        n.E2C[i] = (mine + n.E2C[i].astype(F32)).astype(BF16)
        e2_cross(i).start()

    def e2_total(i):
        e2_cross(i).wait_recv()
        both = n.E2C[i].astype(F32) + n.E2Y[i].astype(F32)
        n.E2P[at(side, high), tokens(i)] = both.astype(BF16)
        e2_last(i).start()

    def scatter_first(C, sems, slot, i):
        targets = (core, corner)
        return [
            copy_to(
                n.PIECES.at[slot, targets[k]], C.at[k, i], sems[0].at[k, i], sems[1].at[k, i], core
            )
            for k in range(2)
        ]

    def scatter_sum(C, first, slot, i):
        for c in first:
            c.wait_recv()
        for k, owner in enumerate((me, across)):
            C[k, i] = (n.PIECES[slot, owner].astype(F32) + C[k, i].astype(F32)).astype(BF16)

    def scatter_cross(C, Y, sems, i):
        return copy_to(C.at[1, i], Y.at[i], sems[0].at[0, i], sems[1].at[0, i], across)

    def b2_first(slot, i):
        return scatter_first(n.B2C, (n.b2c_s, n.b2c_r), slot, i)

    def b2_cross(i):
        return scatter_cross(n.B2C, n.B2Y, (n.b2x_s, n.b2x_r), i)

    def e1_first(slot, i):
        return scatter_first(n.E1C, (n.e1c_s, n.e1c_r), slot, i)

    def e1_cross(i):
        return scatter_cross(n.E1C, n.E1Y, (n.e1x_s, n.e1x_r), i)

    def split(slot, values):
        for p in range(parts):
            n.PIECES[slot, p] = values[p * width : (p + 1) * width]

    def order(step):
        return lax.rem(blocks - step, blocks)

    for i in range(blocks - 1, 0, -1):
        mix.start(i)
        cot.start(i)
    weight.forward()
    mix.forward(0)
    weight.finish()
    n.BM[D:] = jnp.transpose(n.WO[...])

    def middle_block(step, _):
        i = order(step)
        slot = lax.rem(step, 2)

        @pl.when(step == 1)
        def _():
            mix.forward(i)

        mix.finish(i)
        here = tokens(i)
        full, _unused = decompress(n.RES[:, here].astype(F32))
        x1 = full + center(dot(n.BM[D:], n.MIX[:, here]) + col(1))
        n.X1[:, here] = x1
        rows = (x1 * inverse_rms(x1) * col(2)).astype(BF16)
        z = dot(n.WET[...], rows) + col(6)
        square = z * z
        h = 0.5 + 0.5 * jnp.tanh(z * (0.7978845608 + (0.7978845608 * 0.044715) * square))
        active = z * h
        slope = h + active * (1.0 - h) * (
            2 * 0.7978845608 + (6 * 0.7978845608 * 0.044715) * square
        )
        active = active.astype(BF16)
        slope = slope.astype(BF16)
        cot.forward(i)

        @pl.when(step >= 2)
        def _():
            e2_sum(order(step - 1))
            for c in b2_first(slot, order(step - 2)):
                c.wait_send()

        @pl.when(step >= 1)
        def _():
            before = order(step - 1)
            scatter_sum(n.B2C, b2_first(1 - slot, before), 1 - slot, before)

        b2 = dot(n.BT[:D], active[: 2 * width]) + dot(n.BT[D:], active[2 * width :])
        split(slot, center(b2).astype(BF16))
        for c in b2_first(slot, i):
            c.start()
        cot.finish(i)
        g2 = branch_grad(n.COT[:, here].astype(F32)).astype(BF16)
        n.GWR[...] += dot_nt(active, g2)

        @pl.when((step >= 1) & (step < blocks - 1))
        def _():
            mix.forward(order(step + 1))

        d_hidden = (dot(n.WR[...], g2) * slope).astype(BF16)
        n.ACC[...] += dot(g2, pick(0)) + dot(d_hidden, pick(1))
        n.GWE[...] += dot_nt(rows, d_hidden)
        n.E2P[:, here] = dot(n.WE[...], d_hidden).astype(BF16)
        e2_first(i).start()
        return 0

    lax.fori_loop(0, blocks, middle_block, 0)
    last = (blocks - 1) % 2
    for batch in range(2):
        cut = slice(batch * 2 * width, (batch + 1) * 2 * width)
        n.BM[:D, cut] = n.GWE[:, cut].astype(BF16)
        n.BM[D:, cut] = n.GWR[:, cut].astype(BF16)
        feeds[batch].start()
    e2_sum(order(blocks - 1))
    e2_sum(0)
    scatter_sum(n.B2C, b2_first(last, order(blocks - 1)), last, order(blocks - 1))
    for slot, step in ((1 - last, blocks - 2), (last, blocks - 1)):
        for c in b2_first(slot, order(step)):
            c.wait_send()
    n.GWE[...] = jnp.zeros_like(n.GWE)
    n.GWR[...] = jnp.zeros_like(n.GWR)

    def stat_copy(k, i):
        mine = n.STAT.at[me, i]
        return copy_to(mine, mine, n.stat_s.at[k, i], n.stat_r.at[k, i], peers[k])

    stored = rows_of((width, 1)) + me * width < D - 1

    def finish_grad(i):
        here = tokens(i)
        e1_cross(i).wait_recv()
        for k in range(3):
            stat_copy(k, i).wait_recv()
        stat = n.STAT[0, i]
        for p in range(1, parts):
            stat = stat + n.STAT[p, i]
        along, c_last = stat[0:1], stat[1:2]
        inverse, u_last, g_last = n.TOK[i, 0:1], n.TOK[i, 1:2], n.TOK[i, 2:3]
        e1 = n.E1C[0, i].astype(F32) + n.E1Y[i].astype(F32)
        u_own = jnp.where(stored, n.RES[own, here].astype(F32), u_last)
        normed = e1 * u_own * inverse
        n.OWN[:width] += dot(normed.astype(BF16), pick(3))
        cube = inverse * inverse * inverse * along / D
        result = n.X1[at(across, width), here] + inverse * (e1 * own_col(0)) - u_own * cube
        final = g_last + inverse * c_last - u_last * cube
        n.QT[:, here] = jnp.where(stored, result - final, 0.0).astype(BF16)

    def finish_out(i):
        here = tokens(i)
        b2_cross(i).wait_recv()
        b2 = n.B2C[0, i].astype(F32) + n.B2Y[i].astype(F32)
        x2 = n.X1[own, here] + b2 + (own_col(3) - jnp.mean(col(3), axis=0, keepdims=True))
        n.VT[:, here] = jnp.where(stored, x2, 0.0).astype(BF16)
        live = lanes((1, SHORT)) + i * SHORT < total
        n.SQ[me, 0:1] += jnp.where(live, column_sum(x2 * x2), 0.0)

    def service(point):
        quarters = {1: (feed, 0), 2: (feed, 1), 3: (feed, 2), 4: (feed, 3)}
        quarters |= {5: (feed_late, 0), 6: (feed_late, 1), 8: (feed_late, 2), 9: (feed_late, 3)}
        owners = {9: feed, 14: feed_late}
        thirds = {14: (feed, 0)}
        for table, call in (
            (quarters, lambda entry: entry[0].sum_quarter(entry[1])),
            (owners, lambda entry: entry.sum_owners()),
            (thirds, lambda entry: entry[0].forward(entry[1])),
        ):
            for when, entry in table.items():

                @pl.when(point == when)
                def _(call=call, entry=entry):
                    call(entry)

    def backward_block(step, _):
        i = blocks - 1 - step
        slot = lax.rem(step, 2)
        here = tokens(i)

        @pl.when(step == 0)
        def _():
            e2_total(i)

        @pl.when(step == 1)
        def _():
            for b in range(blocks):
                b2_cross(b).start()

        e2_last(i).wait_recv()
        e2_first(i).wait_send()
        n.E2P[at(1 - side, high), here] = n.E2T[i]
        x1 = n.X1[:, here]
        inverse = inverse_rms(x1)
        e2 = n.E2P[:, here].astype(F32)
        normed = e2 * x1
        gain_part = (normed * inverse).astype(BF16)
        along = column_sum(normed * col(2))
        du = inverse * (e2 * col(2)) - x1 * (inverse * inverse * inverse * along / D)
        g1 = branch_grad(n.COT[:, here].astype(F32)) + center(du)
        n.TOK[i, 2:3] = g1[D - 1 :]
        for p in range(parts):

            @pl.when(me == p)
            def _():
                n.X1[at(across, width), here] = g1[p * width : (p + 1) * width]

        g1 = g1.astype(BF16)
        n.ACC[...] += dot(gain_part, pick(2)) + dot(g1, pick(3))
        mixed = n.MIX[own, here]
        n.GW[3 * width :] += dot_nt(mixed, g1)
        d_mixed = dot(n.WO[own], g1).astype(BF16)
        service(5 * step)
        product = d_mixed.astype(F32) * mixed.astype(F32)
        delta = [column_sum(head_rows(product, h)) for h in range(heads)]
        lse = [n.LSE[i, h : h + 1] for h in range(heads)]
        live = i * SHORT < total
        q = n.QT[:, here] * SCORE_SCALE
        q_heads = halves(q)
        g_heads = halves(d_mixed)

        def pair(j, lse, allowed):
            there = tokens(j)
            k_j, v_j, k_t = n.KN[there], n.VN[there], n.KT[:, there]
            dq, dk, dv = [], [], []
            for h in range(heads):
                p = jnp.exp(dot(part_of(k_j, h), q_heads[h]) - lse[h])
                if allowed is not None:
                    p = jnp.where(allowed, p, 0.0)
                dv.append(dot_nt(head_rows(d_mixed, h), p.astype(BF16)))
                p = (p * (dot(part_of(v_j, h), g_heads[h]) - delta[h])).astype(BF16)
                dk.append(dot_nt(head_rows(q, h), p))
                dq.append(dot(head_rows(k_t, h), p))
            n.GWE[at(j, width), :SHORT] += jnp.concatenate(dv, axis=0)
            n.GWR[at(j, width), :SHORT] += jnp.concatenate(dk, axis=0)
            return jnp.concatenate(dq, axis=0)

        dq = pair(i, lse, diagonal(live))

        @pl.when(i >= 1)
        def _():
            e2_total(i - 1)

        service(5 * step + 1)

        @pl.when(step >= 1)
        def _():
            scatter_sum(n.E1C, e1_first(1 - slot, i + 1), 1 - slot, i + 1)
            e1_cross(i + 1).start()

        lse_far = [row + far for row in lse]

        def body(j, dq):
            dq = dq + pair(j, lse_far, None)

            @pl.when(j <= 1)
            def _():
                service(5 * step + 2 + j)

            return dq

        dq = lax.fori_loop(0, i, body, dq)
        d_all = jnp.concatenate(
            [dq * SCORE_SCALE, n.GWR[at(i, width), :SHORT], n.GWE[at(i, width), :SHORT]], axis=0
        ).astype(BF16)
        n.OWN[...] += dot(d_all, pick(0))
        full, inverse = decompress(n.RES[:, here].astype(F32))
        rows = (full * inverse * col(0)).astype(BF16)
        n.GW[: 3 * width] += dot_nt(d_all, rows)
        e1 = dot(n.WN[...], d_all)

        @pl.when(step >= 2)
        def _():
            for c in e1_first(slot, i + 2):
                c.wait_send()

        split(slot, e1.astype(BF16))
        for c in e1_first(slot, i):
            c.start()
        c = e1 * col(0)
        n.STAT[me, i, 0:1] = column_sum(c * full)
        n.STAT[me, i, 1:2] = c[D - 1 :]
        for k in range(3):
            stat_copy(k, i).start()
        n.TOK[i, 0:1] = inverse
        n.TOK[i, 1:2] = full[D - 1 :]
        service(5 * step + 4)
        return 0

    lax.fori_loop(0, blocks, backward_block, 0)
    scatter_sum(n.E1C, e1_first(last, 0), last, 0)
    e1_cross(0).start()
    n.BT[:D] = n.GW[:, : 2 * width].astype(BF16)
    n.BT[D:] = n.GW[:, 2 * width :].astype(BF16)
    rest.start()
    feed.forward(1)
    feed.forward(2)
    for third in range(3):
        feed_late.forward(third)

    def square_copy(k):
        return copy_to(n.SQ.at[me], n.SQ.at[me], n.sq_s.at[k, 0], n.sq_r.at[k, 0], peers[k])

    def finish_block(k, _):
        finish_out(k)
        rest.sum_quarter(k)
        return 0

    lax.fori_loop(0, blocks, finish_block, 0)
    for k in range(3):
        square_copy(k).start()

    def finish_rows(k, _):
        finish_grad(blocks - 1 - k)
        return 0

    lax.fori_loop(0, blocks, finish_rows, 0)
    for k in range(3):
        square_copy(k).wait_recv()

    def tiny_copy(slot, group):
        here = n.SMALL.at[dp]
        return pltpu.make_async_remote_copy(
            src_ref=here,
            dst_ref=here,
            send_sem=n.tiny_s.at[0, group],
            recv_sem=n.tiny_r.at[0, slot],
            device_id={"dp": group},
            device_id_type=MESH,
        )

    squares = jnp.sum(sum(n.SQ[p, 0:1] for p in range(parts)), axis=1, keepdims=True)
    mine = n.ACC[own]
    parts_in = [
        n.OWN[:width, 0:1],
        n.OWN[2 * width :, 0:1],
        n.OWN[:width, 3:4],
        squares,
        mine[:, 3:4],
        mine[:, 2:3],
        mine[:, 0:1],
        total.astype(F32),
    ] + [n.ACC[p * width : (p + 1) * width, 1:2] for p in range(parts)]
    table = jnp.zeros((width, LANES), F32)
    for lane, values in enumerate(parts_in):
        table = jnp.where(lanes(table.shape) == lane, values, table)
    table = jnp.concatenate([table, jnp.zeros((2 * LANES - width, LANES), F32)], axis=0)
    n.SMALL[dp] = jnp.transpose(table)[:16]
    each_group(lambda d, group: tiny_copy(dp, group).start())
    rest.sum_owners()

    def store(src, dst, k):
        return pltpu.make_async_copy(src, dst, n.store_s.at[0, k])

    stores = [store(n.QT, n.grad, 0), store(n.VT, n.out, 1)]
    for c in stores:
        c.start()
    each_group(lambda d, group: tiny_copy(group, group).wait_recv())
    small = n.SMALL[0]
    for group in range(1, groups):
        small = small + n.SMALL[group]
    n.small[...] = small

    def store_batch(batch, target, k):
        batch.finish()

        def body(half, rows):
            store(rows, target.at[half * D : (half + 1) * D], k + half).start()

        batch.take(body)
        for half in range(2):
            here = slice(half * D, (half + 1) * D)
            stores.append(store(batch.buf.at[here], target.at[here], k + half))

    rest.forward(0)
    store_batch(feed, n.feed.at[:, : 2 * width], 2)
    rest.forward(1)
    store_batch(feed_late, n.feed.at[:, 2 * width :], 4)
    rest.forward(2)
    store_batch(rest, n.rest, 6)

    for k in range(3):
        vec_copy(k).wait_send()
        square_copy(k).wait_send()
    weight.drain()

    def drain(i, _):
        for g in (res, cot, mix):
            g.drain(i)
        for c in (e2_cross, e2_last, b2_cross, e1_cross):
            c(i).wait_send()
        for k in range(3):
            stat_copy(k, i).wait_send()
        return 0

    lax.fori_loop(0, blocks, drain, 0)
    for step in (blocks - 2, blocks - 1):
        for c in e1_first(step % 2, blocks - 1 - step):
            c.wait_send()
    for c in stores:
        c.wait()
    for batch in (feed, feed_late, rest):
        batch.drain()
    each_group(lambda d, group: tiny_copy(dp, group).wait_send())


def finish_kernel(
    out, grad, rest_low, rest_high, feed_low, feed_high, small,
    out_ref, grad_ref, gw_ref, gwo_ref, gwe_ref, gwr_ref,
    gb_ref, gbo_ref, gg_one_ref, gg_two_ref, gbe_ref, gbr_ref, rms_ref, live_ref,
):
    i = pl.program_id(0)
    width = gb_ref.shape[1]
    out_ref[...] = out[...]
    grad_ref[...] = grad[...]
    rest = jnp.concatenate([rest_low[...], rest_high[...]], axis=1).astype(F32)
    gwe_ref[...] = feed_low[...].astype(F32)
    gwr_ref[...] = feed_high[...].astype(F32)

    most = pl.num_programs(0) * 3 // 4

    @pl.when(i < most)
    def _():
        gw_ref[...] = rest

    @pl.when(i >= most)
    def _():
        gwo_ref[...] = rest

    @pl.when(i == 0)
    def _():
        gb_ref[...] = small[0:2, :width]
        gg_one_ref[...] = small[2, :width]
        gbo_ref[...] = small[4, :width]
        gg_two_ref[...] = small[5, :width]
        gbr_ref[...] = small[6, :width]
        for p in range(D // width):
            gbe_ref[p * width : (p + 1) * width] = small[8 + p, :width]
        live = small[7:8, 0:1]
        rms_ref[...] = jnp.sqrt(small[3:4, 0:1] / (D * live))
        live_ref[...] = live.astype(jnp.int32)


def on_device(
    residual,
    lengths,
    gain_one,
    input_weight,
    input_bias,
    output_weight,
    output_bias,
    gain_two,
    expand_weight,
    expand_bias,
    reduce_weight,
    reduce_bias,
    cotangent,
):
    count, width = residual.shape
    hidden = expand_weight.shape[1]
    parts = D // width

    def shape(*dims, dtype=F32):
        return jax.ShapeDtypeStruct(dims, dtype)

    groups = lax.axis_size("dp")
    names, scratches = scratch(count, width, hidden, groups)

    def space(name):
        return pl.BlockSpec(memory_space=pltpu.VMEM if name in IN_VMEM else pl.ANY)

    out, grad, rest, feed, small = pl.pallas_call(
        lambda *refs: layer_kernel(groups, names, *refs),
        in_specs=[pl.BlockSpec(memory_space=pltpu.SMEM)] + [space(name) for name in INPUTS[1:]],
        out_specs=[space(name) for name in OUTPUTS],
        out_shape=[
            shape(width, count, dtype=BF16),
            shape(width, count, dtype=BF16),
            shape(2 * D, 2 * width, dtype=BF16),
            shape(2 * D, hidden, dtype=BF16),
            shape(16, 2 * LANES),
        ],
        scratch_shapes=scratches,
        compiler_params=pltpu.CompilerParams(
            vmem_limit_bytes=63 << 20, collective_id=0, has_side_effects=True
        ),
        name="layer",
    )(
        lengths,
        residual.T,
        cotangent.T,
        gain_one[None],
        output_bias[None],
        gain_two[None],
        reduce_bias[None],
        input_bias,
        expand_bias,
        jnp.transpose(input_weight, (0, 2, 1)).reshape(3 * width, D),
        output_weight,
        expand_weight,
        reduce_weight,
    )

    def rows(high, wide, base=0):
        return pl.BlockSpec((high, wide), lambda i: (i + base, 0))

    def whole(*dims):
        return pl.BlockSpec(dims, lambda i: (0,) * len(dims))

    def clip(high, wide, first, last):
        return pl.BlockSpec((high, wide), lambda i: (jnp.clip(i - first, 0, last - first), 0))

    steps = parts
    step = D // steps
    thin = width // steps
    out, grad, gw, gwo, gwe, gwr, *vectors = pl.pallas_call(
        finish_kernel,
        grid=(steps,),
        in_specs=[
            rows(thin, count),
            rows(thin, count),
            rows(step, 2 * width),
            rows(step, 2 * width, steps),
            rows(step, hidden),
            rows(step, hidden, steps),
            whole(16, 2 * LANES),
        ],
        out_specs=[
            rows(thin, count),
            rows(thin, count),
            clip(step, D, 0, steps * 3 // 4 - 1),
            clip(step, D, steps * 3 // 4, steps - 1),
            rows(step, hidden),
            rows(step, hidden),
            whole(2, width),
            whole(width),
            whole(width),
            whole(width),
            whole(hidden),
            whole(width),
            whole(1, 1),
            whole(1, 1),
        ],
        out_shape=[
            shape(width, count, dtype=BF16),
            shape(width, count, dtype=BF16),
            shape(3 * width, D),
            shape(width, D),
            shape(D, hidden),
            shape(hidden, D),
            shape(2, width),
            shape(width),
            shape(width),
            shape(width),
            shape(hidden),
            shape(width),
            shape(1, 1),
            shape(1, 1, dtype=jnp.int32),
        ],
        compiler_params=pltpu.CompilerParams(vmem_limit_bytes=60 << 20),
        name="finish",
    )(out, grad, rest, rest, feed, feed, small)
    gb, gbo, gg_one, gg_two, gbe, gbr, rms, live_count = vectors
    return (
        out.T,
        grad.T,
        jnp.transpose(gw.reshape(3, width, D), (0, 2, 1)),
        gb,
        gwo,
        gbo,
        gg_one,
        gg_two,
        gwe,
        gbe,
        gwr,
        gbr,
        rms[0, 0],
        live_count[0, 0],
    )


def solution(mesh):
    return jax.shard_map(
        on_device,
        mesh=mesh,
        in_specs=(
            P("dp", "mp"),
            P("dp", None),
            P("mp"),
            P(None, None, "mp"),
            P(None, "mp"),
            P("mp", None),
            P("mp"),
            P("mp"),
            P(None, "mp"),
            P("mp"),
            P("mp", None),
            P("mp"),
            P("dp", "mp"),
        ),
        out_specs=(
            P("dp", "mp"),
            P("dp", "mp"),
            P(None, None, "mp"),
            P(None, "mp"),
            P("mp", None),
            P("mp"),
            P("mp"),
            P("mp"),
            P(None, "mp"),
            P("mp"),
            P("mp", None),
            P("mp"),
            P(),
            P(),
        ),
        check_vma=False,
    )
```
